512 devices in a mesh: node: 16 (over z), grp: 8 (over y, core), rep: 4 (over x).
Axes of the slice: x: 4, y: 4, z: 16, core: 2. Of those that a mesh axis runs over, the one named last changes fastest.
Arguments:
- tokens: bfloat16 [16384, 768], P(('node', 'grp'), 'rep'), may hold values from -6 to 6
- gates: float32 [16384, 2], P(('node', 'grp')), may hold values from 0.05 to 1
- expert_ids: int32 [16384, 2], P(('node', 'grp')), may hold values from 0 to 127, all different within a row; in each aligned block of 128 rows (0 to 127, 128 to 255, ...) at most 4 rows name the same one
- w_in: bfloat16 [128, 768, 1536], P(('node', 'grp'), None, 'rep'), may hold values from -0.21875 to 0.21875
- b_in: float32 [128, 1536], P(('node', 'grp'), 'rep'), may hold values from -3 to 3
- w_out: bfloat16 [128, 1536, 768], P(('node', 'grp'), 'rep'), may hold values from -0.15625 to 0.15625
- b_out: float32 [128, 768], P(('node', 'grp'), 'rep'), may hold values from -3 to 3
- cotangent: bfloat16 [16384, 768], P(('node', 'grp'), 'rep'), may hold values from -6 to 6
Outputs:
- mixed: bfloat16 [16384, 768], P(('node', 'grp'), 'rep')
- d_tokens: bfloat16 [16384, 768], P(('node', 'grp'), 'rep')
- d_gates: float32 [16384, 2], P(('node', 'grp'))
- d_w_in: float32 [128, 768, 1536], P(('node', 'grp'), None, 'rep')
- d_b_in: float32 [128, 1536], P(('node', 'grp'), 'rep')
- d_w_out: float32 [128, 1536, 768], P(('node', 'grp'), 'rep')
- d_b_out: float32 [128, 768], P(('node', 'grp'), 'rep')
The draws below stay inside these ranges and needn't reach their ends.
Inputs may be any that keep to these rules, and one draw needn't show every extreme that they name: `expert_ids`: each row names 2 different experts. Among the 128 rows of one device's aligned block no expert is named more than 4 times, and in some blocks one expert is named exactly 4 times.
All inputs are finite; a program needn't handle non-finite values.
Results may differ from the reference program's by a relative error of at most 0.0064.
Values may be sent and summed in bfloat16 or wider, within the bound.
A program may use at most 64 MiB of HBM per device.

```python
import math
import jax
import jax.numpy as jnp
import numpy as np
from jax import lax

D = 768
HID = 1536
TOP = 2
TOK_DEV = 128
EXPERTS = 128
CAP = 4
TOKENS = 16384


def shard_levels(key, shape, pieces, smallest, high):
    loudness, own = 1.0, jax.random.fold_in(key, 6)
    for axis_at, shards_of in pieces:
        draws = jnp.exp(jax.random.uniform(jax.random.fold_in(own, axis_at), (shards_of,), jnp.float32, smallest / len(pieces), high / len(pieces)))
        loudness = loudness * jnp.repeat(draws, shape[axis_at] // shards_of).reshape([-1 if axis == axis_at else 1 for axis in range(len(shape))])
    return loudness


def deal_out(own_key, own, number, rows, number_of, top, reach, skew):
    ranking = jax.random.permutation(own_key, number_of)
    crowded, usual = load_shares(number_of, rows * top, reach, skew, True), load_shares(number_of, rows * top, reach, skew, False)
    places = jnp.arange(number_of)

    def named(lengths, offset_by):
        used = int((lengths > 0).sum())
        fixed = max(1, used // 4)
        shifted = fixed + (places - fixed + offset_by * (used - fixed)) % max(1, number_of - fixed)
        return jnp.zeros((number_of,), jnp.int32).at[ranking[jnp.where(places < fixed, places, shifted)]].set(jnp.asarray(lengths, jnp.int32))

    lengths = jnp.where(number % 4 == 0, named(crowded, number // 4), named(usual, number - number // 4 - 1))
    mixed = jax.random.permutation(jax.random.fold_in(own, 3), number_of)
    giver, sink = mixed[0:number_of // 2 * 2:2], mixed[1:number_of // 2 * 2:2]
    slack = jnp.minimum(lengths[giver] - 1, reach - lengths[sink]) // 2
    slack = jnp.where((giver == ranking[0]) | (sink == ranking[0]) | (lengths[sink] == 0), 0, jnp.maximum(slack, 0))
    shifted = jax.random.randint(jax.random.fold_in(own, 4), (number_of // 2,), 0, 1 << 20) % (slack + 1)
    lengths = lengths.at[giver].add(-shifted).at[sink].add(shifted)
    items = jnp.searchsorted(jnp.cumsum(lengths), jnp.arange(rows * top), side="right").astype(jnp.int32)
    grid = items.reshape(top, rows).T
    grid = grid[jax.random.permutation(jax.random.fold_in(own, 1), rows)]
    offset_by = jax.random.randint(jax.random.fold_in(own, 2), (rows, 1), 0, top)
    return jnp.take_along_axis(grid, (jnp.arange(top)[None, :] + offset_by) % top, axis=1)


def load_shares(count, total, limit, slope, full):
    weights = [(1 << 20) // math.isqrt(rank ** slope) + 1 for rank in range(1, count + 1)]
    largest = limit if full else min(limit, max(-(-total // count), total * weights[0] // sum(weights)))
    least = 1 if total - largest >= count - 1 else 0
    holding, spare = [largest] + [least] * (count - 1), total - largest - least * (count - 1)
    while spare > 0:
        free = [i for i in range(1, count) if holding[i] < largest] or [i for i in range(1, count) if holding[i] < limit]
        pool, budget = sum([weights[i] for i in free]), spare
        for i in free:
            addition = min(limit - holding[i], max(1, budget * weights[i] // pool), spare)
            holding[i] = holding[i] + addition
            spare = spare - addition
    return np.array(holding)


def scatter_about(own_key, extent, scale, most, pieces=(), held_as=jnp.bfloat16):
    array = scale * jax.random.normal(own_key, extent, jnp.float32)
    if pieces:
        array = array * shard_levels(own_key, extent, pieces, -0.22, 0.18)
    return jnp.clip(array, -most, most).astype(held_as)


def setup_inputs(seed: int = 0) -> dict:
    splits = jax.random.split(jax.random.key(seed), 9)
    tokens = scatter_about(splits[0], (TOKENS, D), 1.0, 6.0, ((0, 128), (1, 4)))
    gates = jnp.clip(jnp.exp(math.log(1.0) - 2.9957323 * jax.random.uniform(splits[1], (TOKENS, TOP), jnp.float32) ** shard_levels(splits[1], (TOKENS, TOP), ((0, 128),), -0.2, 0.2)), 0.05, 1.0)
    expert_ids_keys = jax.random.split(jax.random.fold_in(splits[2], 1), TOKENS // TOK_DEV)
    expert_ids_turns = jax.random.permutation(jax.random.fold_in(splits[2], 3), TOKENS // TOK_DEV)
    expert_ids = jax.vmap(lambda own, number: deal_out(jax.random.fold_in(splits[2], 2), own, number, TOK_DEV, EXPERTS, TOP, CAP, 2))(expert_ids_keys, expert_ids_turns).reshape((TOKENS, TOP))
    w_in = scatter_about(splits[3], (EXPERTS, D, HID), D ** -0.5, 0.21875, ((0, 128), (2, 4)))
    b_in = scatter_about(splits[4], (EXPERTS, HID), 0.5, 3.0, ((0, 128), (1, 4)), jnp.float32)
    w_out = scatter_about(splits[5], (EXPERTS, HID, D), HID ** -0.5, 0.15625, ((0, 128), (1, 4)))
    b_out = scatter_about(splits[6], (EXPERTS, D), 0.5, 3.0, ((0, 128), (1, 4)), jnp.float32)
    cotangent = scatter_about(splits[7], (TOKENS, D), 1.0, 6.0, ((0, 128), (1, 4)))
    return dict(tokens=tokens, gates=gates, expert_ids=expert_ids, w_in=w_in, b_in=b_in, w_out=w_out, b_out=b_out, cotangent=cotangent)


def slot_ranks(row_ids):
    position = jnp.arange(row_ids.shape[0], dtype=jnp.int32)
    matches = (row_ids[:, None] == row_ids[None, :]) & (position[None, :] < position[:, None])
    return lax.optimization_barrier(jnp.sum(matches.astype(jnp.int32), axis=1)).astype(jnp.int32)

def pick_rows(source_rows, index, filled):
    safe_index = jnp.where(filled, index, 0).astype(jnp.int32)
    return jnp.where(filled[:, None], source_rows[safe_index], 0).astype(source_rows.dtype)

def contract_first(left, right):
    return lax.dot_general(left, right, (((0,), (0,)), ((), ())), preferred_element_type=jnp.float32)

def contract_last(left, right):
    return lax.dot_general(left, right, (((1,), (1,)), ((), ())), preferred_element_type=jnp.float32)

def reference(tokens, gates, expert_ids, w_in, b_in, w_out, b_out, cotangent):
    assigned = TOK_DEV * TOP
    blocks = expert_ids.reshape(EXPERTS, assigned).astype(jnp.int32)
    slot_rank = jax.vmap(slot_ranks)(blocks)
    source = jnp.arange(EXPERTS, dtype=jnp.int32)[:, None]
    target = ((blocks * EXPERTS + source) * CAP + slot_rank).reshape(-1).astype(jnp.int32)
    total_slots = EXPERTS * EXPERTS * CAP
    owner = jnp.full((total_slots,), -1, jnp.int32).at[target].set(jnp.arange(TOKENS * TOP, dtype=jnp.int32))
    owner = owner.reshape(EXPERTS, EXPERTS * CAP)

    def expert_forward(operands):
        slot_owner, w_first, bias_first, w_second, bias_second = operands
        filled = slot_owner >= 0
        expert_rows = pick_rows(tokens, slot_owner // TOP, filled)
        pre_act = jnp.dot(expert_rows, w_first, preferred_element_type=jnp.float32) + bias_first
        hidden = jax.nn.gelu(pre_act).astype(jnp.bfloat16)
        return (jnp.dot(hidden, w_second, preferred_element_type=jnp.float32) + bias_second).astype(jnp.bfloat16)
    expert_out = lax.map(expert_forward, (owner, w_in, b_in, w_out, b_out)).reshape(total_slots, D)
    per_assign = expert_out[target].reshape(TOKENS, TOP, D).astype(jnp.float32)
    mixed = lax.optimization_barrier(jnp.sum(gates[:, :, None] * per_assign, axis=1)).astype(jnp.bfloat16)
    cot_wide = cotangent.astype(jnp.float32)
    d_gates = lax.optimization_barrier(jnp.sum(cot_wide[:, None, :] * per_assign, axis=2))
    d_out = (gates[:, :, None] * cot_wide[:, None, :]).astype(jnp.bfloat16).reshape(TOKENS * TOP, D)

    def expert_backward(operands):
        slot_owner, w_first, bias_first, w_second = operands
        filled = slot_owner >= 0
        expert_rows = pick_rows(tokens, slot_owner // TOP, filled)
        grad_rows = pick_rows(d_out, slot_owner, filled)
        pre_act = jnp.dot(expert_rows, w_first, preferred_element_type=jnp.float32) + bias_first
        hidden = jax.nn.gelu(pre_act).astype(jnp.bfloat16)
        grad_bias_out = lax.optimization_barrier(jnp.sum(grad_rows.astype(jnp.float32), axis=0))
        grad_w_out = contract_first(hidden, grad_rows)
        d_hidden = contract_last(grad_rows, w_second)
        _, pull_back = jax.vjp(jax.nn.gelu, pre_act)
        d_pre = pull_back(d_hidden)[0].astype(jnp.bfloat16)
        grad_bias_in = lax.optimization_barrier(jnp.sum(d_pre.astype(jnp.float32), axis=0))
        grad_w_in = contract_first(expert_rows, d_pre)
        d_row = contract_last(d_pre, w_first).astype(jnp.bfloat16)
        return (d_row, grad_w_in, grad_bias_in, grad_w_out, grad_bias_out)
    d_row, d_w_in, d_b_in, d_w_out, d_b_out = lax.map(expert_backward, (owner, w_in, b_in, w_out))
    row_grads = d_row.reshape(total_slots, D)[target].reshape(TOKENS, TOP, D).astype(jnp.float32)
    d_tokens = lax.optimization_barrier(jnp.sum(row_grads, axis=1)).astype(jnp.bfloat16)
    return (mixed, d_tokens, d_gates, d_w_in, d_b_in, d_w_out, d_b_out)
```

```python
import functools
import math

import jax
import jax.numpy as jnp
from jax import lax
from jax.experimental import pallas as pl
from jax.experimental.pallas import tpu as pltpu
from jax.sharding import PartitionSpec as P

MESH = pl.DeviceIdType.MESH
CAP = 4
BF = jnp.bfloat16
F32 = jnp.float32
ROOT = math.sqrt(2.0 / math.pi)


def dot(a, b, ca, cb):
    return lax.dot_general(a, b, (((ca,), (cb,)), ((), ())), preferred_element_type=F32)


def fused(
    N, G, R,
    tok, cot, ids, gates, w_in, b_in, w_out, b_out,
    mixed, d_tok, d_gates, d_w_in, d_b_in, d_w_out, d_b_out,
    zt, zc, zm, onehot, ysend, yrecv, xall, w_out_t, pre, dgelu, hid, d_pre,
    xhalf, xfull, rhalf, rfull, back, yret, zs, zr, gs, gr, dsum, drecv,
    z_send, z_recv, y_send, y_recv, x_send, x_recv, r_send, r_recv,
    b_send, b_recv, s_send, s_recv, p_send, p_recv,
):
    n, g, r = lax.axis_index("node"), lax.axis_index("grp"), lax.axis_index("rep")
    F, T = tok.shape
    D, H = w_in.shape
    U = N // 2
    V = U // 2
    Q = V * 8
    S = 2 * G * Q
    HF, FB = F // 2, F - 128

    def at(axis, index):
        return {axis: index}

    right_z, left_z = lax.rem(n + 1, N), lax.rem(n + N - 1, N)
    right_x, left_x = lax.rem(r + 1, R), lax.rem(r + R - 1, R)
    far_x = lax.rem(r + 2, R)

    barrier = pltpu.get_barrier_semaphore()
    peers = [at("node", right_z), at("node", left_z)]
    peers += [at("grp", lax.rem(g + j, G)) for j in range(1, G)]
    peers += [at("rep", lax.rem(r + j, R)) for j in range(1, R)]
    for peer in peers:
        pl.semaphore_signal(barrier, inc=1, device_id=peer, device_id_type=MESH)
    pl.semaphore_wait(barrier, len(peers))

    def remote(src, dst, send, recv, peer):
        return pltpu.make_async_remote_copy(
            src_ref=src, dst_ref=dst, send_sem=send, recv_sem=recv,
            device_id=peer, device_id_type=MESH,
        )

    @functools.cache
    def z_copies(which, d):
        own, buf = ((tok, zt), (cot, zc), (None, zm))[which]
        src_r = buf.at[N - d + 1] if d > 1 else (own if which < 2 else buf.at[0])
        src_l = buf.at[d - 1] if d > 1 else (own if which < 2 else buf.at[0])
        if d < U:
            right = (src_r, buf.at[N - d])
            left = (src_l, buf.at[d])
        elif which < 2:
            right = (src_r.at[pl.ds(0, HF)], buf.at[U, pl.ds(0, HF)])
            left = (src_l.at[pl.ds(HF, HF)], buf.at[U, pl.ds(HF, HF)])
        else:
            right, left = (src_r, buf.at[U]), None
        found = [
            remote(*right, z_send.at[which, 0, d - 1], z_recv.at[which, 0, d - 1], at("node", right_z))
        ]
        if left is not None:
            found.append(
                remote(*left, z_send.at[which, 1, d - 1], z_recv.at[which, 1, d - 1], at("node", left_z))
            )
        return found

    started = []

    def start(copies):
        for copy in copies:
            copy.start()
        started.extend(copies)

    start(z_copies(0, 1) + z_copies(1, 1))

    ids_f = ids[...].astype(F32)
    rows = [ids_f[k : k + 1, :] for k in range(2)]
    cols = [jnp.broadcast_to(row, (T, T)).T for row in rows]
    earlier = lax.broadcasted_iota(jnp.int32, (T, T), 0) < lax.broadcasted_iota(jnp.int32, (T, T), 1)
    meta = []
    for k in range(2):
        same = jnp.where(cols[0] == rows[k], 1.0, 0.0) + jnp.where(cols[1] == rows[k], 1.0, 0.0)
        rank = jnp.sum(jnp.where(earlier, same, 0.0), axis=0, keepdims=True)
        meta.append(rows[k] * CAP + rank)
    zm[0] = jnp.concatenate(
        meta + [gates[0:1, :], gates[1:2, :], jnp.zeros((4, T), F32)], axis=0
    )
    start(z_copies(2, 1))

    row = lax.broadcasted_iota(jnp.int32, (G * 8, T), 0)
    inner = lax.rem(row, 8)
    code = (n * G + row // 8) * CAP + lax.rem(inner, 4)
    codes = [jnp.where(inner // 4 == p, code, -1).astype(F32) for p in range(2)]

    w_out_t[...] = w_out[...].T

    def pair(u):
        return (u + 1, N - u - 1) if u < U - 1 else (0, U)

    def select(u):
        h, v = u // V, u % V
        slots = pair(u)
        info = [zm[s] for s in slots]
        hot = []
        weight = jnp.zeros((G * 8, 1), F32)
        for k in range(2):
            parts = [jnp.where(info[p][k : k + 1, :] == codes[p], 1.0, 0.0) for p in range(2)]
            for p in range(2):
                weight += jnp.sum(parts[p] * info[p][2 + k : 3 + k, :], axis=1, keepdims=True)
            both = jnp.concatenate(parts, axis=1)
            hot.append(both)
            onehot[u, k] = both.astype(BF)
        place = (hot[0] + hot[1]).astype(BF)
        for which, buf in ((0, zt), (1, zc)):
            got = None
            for p, slot in enumerate(slots):
                block = (tok, cot)[which][...] if slot == 0 else buf[slot]
                part = dot(place[:, p * T : (p + 1) * T], block, 1, 1)
                got = part if got is None else got + part
            if which == 1:
                got = got * weight
            got = got.reshape(G, 8, F)
            ysend[which, :, h, v * 8 : v * 8 + 8, :] = got[:, :, 0:128].astype(BF)
            ysend[which, :, 2, v * 8 : v * 8 + 8, h * FB : (h + 1) * FB] = got[:, :, 128:F].astype(BF)

    for d in range(1, U + 1):
        for which in (2, 0, 1):
            for copy in z_copies(which, d):
                copy.wait_recv()
            if d < U:
                start(z_copies(which, d + 1))
        select(d - 1)

    @functools.cache
    def y_copies(which):
        return [
            remote(
                ysend.at[which, lax.rem(g + j, G)], yrecv.at[which, :, g],
                y_send.at[which, j - 1], y_recv.at[which, j - 1], at("grp", lax.rem(g + j, G)),
            )
            for j in range(1, G)
        ]

    for which in range(2):
        start(y_copies(which))
    for which in range(2):
        yrecv[which, :, g] = ysend[which, g]

    @functools.cache
    def x_near(which):
        own = xall.at[which, r]
        return [
            remote(own, own, x_send.at[which, 0], x_recv.at[which, 0], at("rep", right_x)),
            remote(own, own, x_send.at[which, 1], x_recv.at[which, 1], at("rep", left_x)),
        ]

    @functools.cache
    def x_relay(which):
        top = xall.at[which, left_x, pl.ds(0, HF)]
        low = xall.at[which, right_x, pl.ds(HF, HF)]
        return [
            remote(top, top, x_send.at[which, 2], x_recv.at[which, 2], at("rep", right_x)),
            remote(low, low, x_send.at[which, 3], x_recv.at[which, 3], at("rep", left_x)),
        ]

    def unpack(which):
        rows_of = G * Q
        for h in range(2):
            xall[which, r, 0:128, h * rows_of : (h + 1) * rows_of] = (
                yrecv[which, h].reshape(rows_of, 128).T
            )
        low = yrecv[which, 2].reshape(rows_of, 128).T
        for h in range(2):
            xall[which, r, 128:F, h * rows_of : (h + 1) * rows_of] = low[h * FB : (h + 1) * FB]

    for which in range(2):
        for copy in y_copies(which):
            copy.wait_recv()
        unpack(which)
        start(x_near(which))

    def relay(which):
        near, passed = x_near(which), x_relay(which)
        for i in range(2):
            near[i].wait_recv()
            start([passed[i]])

    def arrive(which):
        for copy in x_relay(which):
            copy.wait_recv()

    relay(0)
    arrive(0)
    x_full = xall[0].reshape(D, S)
    bias = jnp.broadcast_to(b_in[...], (128, H)).T
    acc = dot(w_in[...], x_full, 0, 0)
    acc = acc + jnp.concatenate([bias] * (S // 128), axis=1) if S >= 128 else acc + bias[:, :S]
    t = jnp.tanh(ROOT * (acc + 0.044715 * acc * acc * acc))
    hid[...] = (0.5 * acc * (1.0 + t)).astype(BF)
    dgelu[...] = 0.5 * (1.0 + t) + 0.5 * acc * (1.0 - t * t) * (ROOT * (1.0 + 3 * 0.044715 * acc * acc))
    relay(1)

    @functools.cache
    def half_copies(way):
        return [
            remote(xhalf.at[way, 0], rhalf.at[way, 0], r_send.at[way, 0], r_recv.at[way, 0], at("rep", left_x)),
            remote(xhalf.at[way, 1], rhalf.at[way, 1], r_send.at[way, 1], r_recv.at[way, 1], at("rep", right_x)),
        ]

    @functools.cache
    def full_copies(way):
        return [
            remote(xfull.at[way, 0], rfull.at[way, 0], r_send.at[way, 2], r_recv.at[way, 2], at("rep", left_x)),
            remote(xfull.at[way, 1], rfull.at[way, 1], r_send.at[way, 3], r_recv.at[way, 3], at("rep", right_x)),
        ]

    def partial(way, target):
        span = pl.ds(pl.multiple_of(target * F, F), F)
        return dot(w_out_t[span, :], hid[...], 1, 0) if way == 0 else dot(w_in[span, :], d_pre[...], 1, 0)

    def scatter_start(way):
        far = partial(way, far_x).astype(BF)
        xhalf[way, 0] = far[0:HF]
        xhalf[way, 1] = far[HF:F]
        start(half_copies(way))

    def scatter_middle(way):
        halves = half_copies(way)
        for i, target in ((0, left_x), (1, right_x)):
            mine = partial(way, target)
            halves[i].wait_recv()
            came = rhalf[way, i].astype(F32)
            if i == 0:
                xfull[way, i] = jnp.concatenate([mine[0:HF] + came, mine[HF:F]], axis=0).astype(BF)
            else:
                xfull[way, i] = jnp.concatenate([mine[0:HF], mine[HF:F] + came], axis=0).astype(BF)
            start([full_copies(way)[i]])

    def scatter_end(way):
        total = partial(way, r)
        for i, copy in enumerate(full_copies(way)):
            copy.wait_recv()
            total = total + rfull[way, i].astype(F32)
        return total

    @functools.cache
    def b_copies(way):
        return [
            remote(
                back.at[way, lax.rem(g + j, G)], yret.at[way, :, g],
                b_send.at[way, j - 1], b_recv.at[way, j - 1], at("grp", lax.rem(g + j, G)),
            )
            for j in range(1, G)
        ]

    def give_back(way, total):
        rows_of = G * Q
        value = total.astype(BF)
        low = jnp.concatenate([value[128:F, h * rows_of : (h + 1) * rows_of] for h in range(2)], axis=0)
        pieces = [value[0:128, h * rows_of : (h + 1) * rows_of] for h in range(2)] + [low]
        for i, piece in enumerate(pieces):
            back[way, :, i] = piece.T.reshape(G, Q, 128)
        start(b_copies(way))
        yret[way, :, g] = back[way, g]

    scatter_start(0)
    arrive(1)
    g_full = xall[1].reshape(D, S)
    slope = dot(w_out[...], g_full, 1, 0)
    d_pre[...] = (slope * dgelu[...]).astype(BF)
    scatter_middle(0)
    scatter_start(1)
    out_bias = jnp.broadcast_to(b_out[...], (128, F)).T
    wide = jnp.concatenate([out_bias] * (S // 128), axis=1) if S >= 128 else out_bias[:, :S]
    give_back(0, scatter_end(0) + wide)
    scatter_middle(1)

    @functools.cache
    def s_copies(way, i):
        found = []
        for side, peer in ((0, right_z), (1, left_z)):
            src, dst = zs.at[way, side, i], zr.at[way, side, i]
            if i == 0:
                span = pl.ds(side * HF, HF)
                src, dst = src.at[span], dst.at[span]
            found.append(remote(src, dst, s_send.at[way, side, i], s_recv.at[way, side, i], at("node", peer)))
        return found

    @functools.cache
    def m_copies(i):
        return [
            remote(gs.at[side, i], gr.at[side, i], s_send.at[2, side, i], s_recv.at[2, side, i], at("node", peer))
            for side, peer in ((0, right_z), (1, left_z))
        ]

    def returned(way, u):
        h, v = u // V, u % V
        a = yret[way, h, :, v * 8 : v * 8 + 8, :].reshape(G * 8, 128)
        b = yret[way, 2, :, v * 8 : v * 8 + 8, :].reshape(G * 8, 128)
        both = jnp.concatenate([a, b], axis=1)
        if way == 0:
            hot = [onehot[u, 0], onehot[u, 1]]
        else:
            hot = [onehot[u, 0] + onehot[u, 1]]
        results = []
        for one in hot:
            full = dot(both, one, 0, 0)
            results.append(jnp.concatenate([full[0:128], full[128 + h * FB : 128 + (h + 1) * FB]], axis=0))
        out = []
        for p, slot in enumerate(pair(u)):
            cut = [one[:, p * T : (p + 1) * T] for one in results]
            if way == 1:
                out.append((cut[0], None))
                continue
            info = zm[slot]
            sent = (cot[...] if slot == 0 else zc[slot]).astype(F32)
            value = info[2:3, :] * cut[0] + info[3:4, :] * cut[1]
            sums = [jnp.sum(one * sent, axis=0, keepdims=True) for one in cut]
            out.append((value, jnp.concatenate(sums + [jnp.zeros((6, T), F32)], axis=0)))
        return out

    def ring(way):
        (home, home_g), (value, sums) = returned(way, U - 1)
        for side in range(2):
            zs[way, side, 0] = value.astype(BF)
        start(s_copies(way, 0))
        if way == 0:
            gs[0, 0] = sums
            gs[1, 0] = jnp.zeros((8, T), F32)
            start(m_copies(0))
        for i in range(1, U):
            ahead, behind = returned(way, U - 1 - i)
            before = s_copies(way, i - 1)
            for side, (value, sums) in enumerate((ahead, behind)):
                before[side].wait_recv()
                came = zr[way, side, i - 1]
                if i == 1:
                    came = came.astype(F32)
                    lo, hi = value[0:HF], value[HF:F]
                    if side == 0:
                        total = jnp.concatenate([lo + came[0:HF], hi], axis=0)
                    else:
                        total = jnp.concatenate([lo, hi + came[HF:F]], axis=0)
                else:
                    total = value + came.astype(F32)
                zs[way, side, i] = total.astype(BF)
                start([s_copies(way, i)[side]])
                if way == 0:
                    m_copies(i - 1)[side].wait_recv()
                    gs[side, i] = sums + gr[side, i - 1]
                    start([m_copies(i)[side]])
        last = s_copies(way, U - 1)
        total = home
        for side in range(2):
            last[side].wait_recv()
            total = total + zr[way, side, U - 1].astype(F32)
            if way == 0:
                m_copies(U - 1)[side].wait_recv()
                home_g = home_g + gr[side, U - 1]
        return total, home_g

    for copy in b_copies(0):
        copy.wait_recv()
    total, sums = ring(0)
    mixed[...] = total.astype(BF)
    dsum[...] = sums
    shares = [
        remote(dsum, drecv.at[j - 1], p_send.at[j - 1], p_recv.at[j - 1], at("rep", lax.rem(r + j, R)))
        for j in range(1, R)
    ]
    start(shares)

    give_back(1, scatter_end(1))

    ones = jnp.ones((8, S), BF)
    d_w_in[...] = dot(xall[0].reshape(D, S), d_pre[...], 1, 1)
    d_w_out[...] = dot(hid[...], xall[1].reshape(D, S), 1, 1)
    d_b_in[...] = dot(ones, d_pre[...], 1, 1)[0:1]
    d_b_out[...] = dot(ones, xall[1, r], 1, 1)[0:1]

    for copy in b_copies(1):
        copy.wait_recv()
    total, _ = ring(1)
    d_tok[...] = total.astype(BF)
    for j, copy in enumerate(shares):
        copy.wait_recv()
        sums = sums + drecv[j]
    d_gates[...] = sums[0:2]
    for copy in started:
        copy.wait_send()


def per_device(tokens, gates, expert_ids, w_in, b_in, w_out, b_out, cotangent):
    N, G, R = lax.axis_size("node"), lax.axis_size("grp"), lax.axis_size("rep")
    T, F = tokens.shape
    _, D, H = w_in.shape
    U = N // 2
    V = U // 2
    Q = V * 8
    S = 2 * G * Q
    HF = F // 2
    dma = pltpu.SemaphoreType.DMA
    vmem = pl.BlockSpec(memory_space=pltpu.VMEM)
    out = pl.pallas_call(
        functools.partial(fused, N, G, R),
        out_shape=(
            jax.ShapeDtypeStruct((F, T), BF),
            jax.ShapeDtypeStruct((F, T), BF),
            jax.ShapeDtypeStruct((2, T), F32),
            jax.ShapeDtypeStruct((D, H), F32),
            jax.ShapeDtypeStruct((1, H), F32),
            jax.ShapeDtypeStruct((H, D), F32),
            jax.ShapeDtypeStruct((1, F), F32),
        ),
        in_specs=[vmem] * 8,
        out_specs=(vmem,) * 7,
        scratch_shapes=[
            pltpu.VMEM((N, F, T), BF),
            pltpu.VMEM((N, F, T), BF),
            pltpu.VMEM((N, 8, T), F32),
            pltpu.VMEM((U, 2, G * 8, 2 * T), BF),
            pltpu.VMEM((2, G, 3, Q, 128), BF),
            pltpu.VMEM((2, 3, G, Q, 128), BF),
            pltpu.VMEM((2, R, F, S), BF),
            pltpu.VMEM((D, H), BF),
            pltpu.VMEM((8, 128), F32),
            pltpu.VMEM((H, S), F32),
            pltpu.VMEM((H, S), BF),
            pltpu.VMEM((H, S), BF),
            pltpu.VMEM((2, 2, HF, S), BF),
            pltpu.VMEM((2, 2, F, S), BF),
            pltpu.VMEM((2, 2, HF, S), BF),
            pltpu.VMEM((2, 2, F, S), BF),
            pltpu.VMEM((2, G, 3, Q, 128), BF),
            pltpu.VMEM((2, 3, G, Q, 128), BF),
            pltpu.VMEM((2, 2, U, F, T), BF),
            pltpu.VMEM((2, 2, U, F, T), BF),
            pltpu.VMEM((2, U, 8, T), F32),
            pltpu.VMEM((2, U, 8, T), F32),
            pltpu.VMEM((8, T), F32),
            pltpu.VMEM((R - 1, 8, T), F32),
            dma((3, 2, U)),
            dma((3, 2, U)),
            dma((2, G - 1)),
            dma((2, G - 1)),
            dma((2, 4)),
            dma((2, 4)),
            dma((2, 4)),
            dma((2, 4)),
            dma((2, G - 1)),
            dma((2, G - 1)),
            dma((3, 2, U)),
            dma((3, 2, U)),
            dma((R - 1,)),
            dma((R - 1,)),
        ],
        compiler_params=pltpu.CompilerParams(
            collective_id=0, has_side_effects=True, vmem_limit_bytes=60 * 2**20
        ),
    )(
        tokens.T, cotangent.T, expert_ids.T, gates.T,
        w_in[0], b_in, w_out[0], b_out,
    )
    mixed, d_tok, d_gates, d_w_in, d_b_in, d_w_out, d_b_out = out
    return (mixed.T, d_tok.T, d_gates.T, d_w_in[None], d_b_in, d_w_out[None], d_b_out)


def solution(mesh):
    both = ("node", "grp")
    return jax.shard_map(
        per_device,
        mesh=mesh,
        in_specs=(
            P(both, "rep"),
            P(both, None),
            P(both, None),
            P(both, None, "rep"),
            P(both, "rep"),
            P(both, "rep", None),
            P(both, "rep"),
            P(both, "rep"),
        ),
        out_specs=(
            P(both, "rep"),
            P(both, "rep"),
            P(both, None),
            P(both, None, "rep"),
            P(both, "rep"),
            P(both, "rep", None),
            P(both, "rep"),
        ),
        check_vma=False,
    )
```

```python
import functools
import math

import jax
import jax.numpy as jnp
from jax import lax
from jax.experimental import pallas as pl
from jax.experimental.pallas import tpu as pltpu
from jax.sharding import PartitionSpec as P

MESH = pl.DeviceIdType.MESH
CAP = 4
BF = jnp.bfloat16
F32 = jnp.float32
ROOT = math.sqrt(2.0 / math.pi)


def dot(a, b, ca, cb):
    return lax.dot_general(a, b, (((ca,), (cb,)), ((), ())), preferred_element_type=F32)


def fused(
    N, G, R,
    tok, cot, ids, gates, w_in, b_in, w_out, b_out,
    mixed, d_tok, d_gates, d_w_in, d_b_in, d_w_out, d_b_out,
    zsend, zrecv, place, ysend, yrecv, xall, w_out_t, dgelu, hid, d_pre,
    xhalf, xfull, rhalf, rfull, back, yret, zback, zret, grad_in, grad_out, dsum, drecv,
    z_send, z_recv, y_send, y_recv, x_send, x_recv, r_send, r_recv,
    b_send, b_recv, s_send, s_recv, p_send, p_recv, o_sem,
):
    n, g, r = lax.axis_index("node"), lax.axis_index("grp"), lax.axis_index("rep")
    F, T = tok.shape
    D, H = w_in.shape
    A = G * CAP
    B = A // 2
    K = N // 4
    Q = 2 * N
    S = 2 * G * Q
    HF, FB = F // 2, F - 128
    C = G // 2

    right_x, left_x = lax.rem(r + 1, R), lax.rem(r + R - 1, R)
    far_x = lax.rem(r + 2, R)

    barrier = pltpu.get_barrier_semaphore()
    peers = [{"node": lax.rem(n + j, N)} for j in range(1, N)]
    peers += [{"grp": lax.rem(g + j, G)} for j in range(1, G)]
    peers += [{"rep": lax.rem(r + j, R)} for j in range(1, R)]
    for peer in peers:
        pl.semaphore_signal(barrier, inc=1, device_id=peer, device_id_type=MESH)

    def remote(src, dst, send, recv, peer):
        return pltpu.make_async_remote_copy(
            src_ref=src, dst_ref=dst, send_sem=send, recv_sem=recv,
            device_id=peer, device_id_type=MESH,
        )

    started = []

    def start(copies):
        for copy in copies:
            copy.start()
        started.extend(copies)

    def arrived(copies):
        for copy in copies:
            copy.wait_recv()

    ids_f = ids[...].astype(F32)
    rows = [ids_f[k : k + 1, :] for k in range(2)]
    cols = [jnp.broadcast_to(row, (T, T)).T for row in rows]
    earlier = lax.broadcasted_iota(jnp.int32, (T, T), 0) < lax.broadcasted_iota(jnp.int32, (T, T), 1)
    slot = lax.broadcasted_iota(jnp.int32, (N * A, T), 0).astype(F32)
    for k in range(2):
        same = jnp.where(cols[0] == rows[k], 1.0, 0.0) + jnp.where(cols[1] == rows[k], 1.0, 0.0)
        rank = jnp.sum(jnp.where(earlier, same, 0.0), axis=0, keepdims=True)
        target = rows[k] * CAP + rank
        place[:, k * T : (k + 1) * T] = jnp.where(slot == target, 1.0, 0.0).astype(BF)

    order = [N // 2]
    for j in range(N // 2 - 1, 0, -1):
        order += [j, N - j]

    @functools.cache
    def z_copies(which):
        return [
            remote(
                zsend.at[which, lax.rem(n + j, N)], zrecv.at[which, n],
                z_send.at[which, j - 1], z_recv.at[which, j - 1], {"node": lax.rem(n + j, N)},
            )
            for j in order
        ]

    def lay(which):
        if which == 0:
            got = dot(place[:, 0:T] + place[:, T : 2 * T], tok[...], 1, 1)
        else:
            wide = cot[...].astype(F32)
            grads = [(gates[k : k + 1, :] * wide).astype(BF) for k in range(2)]
            got = dot(place[...], jnp.concatenate(grads, axis=1), 1, 1)
        got = got.reshape(N, A, F)
        zsend[which, :, 0:A, :] = got[:, :, 0:128].astype(BF)
        for c in range(2):
            zsend[which, :, A : A + B, c * FB : (c + 1) * FB] = got[:, c * B : (c + 1) * B, 128:F].astype(BF)

    lay(0)
    pl.semaphore_wait(barrier, len(peers))
    start(z_copies(0))
    lay(1)
    start(z_copies(1))
    for which in range(2):
        zrecv[which, n] = zsend[which, n]

    def shuffle(experts):
        size = 4 * experts * CAP
        i = lax.broadcasted_iota(jnp.int32, (size, size), 0)
        j = lax.broadcasted_iota(jnp.int32, (size, size), 1)
        e, v, s = i // (4 * CAP), lax.rem(i // CAP, 4), lax.rem(i, CAP)
        return jnp.where(j == (v * experts + e) * CAP + s, 1.0, 0.0).astype(BF)

    mix_a, mix_b = shuffle(G), shuffle(C)

    @functools.cache
    def y_copies(which):
        return [
            remote(
                ysend.at[which, lax.rem(g + j, G)], yrecv.at[which, :, g],
                y_send.at[which, j - 1], y_recv.at[which, j - 1], {"grp": lax.rem(g + j, G)},
            )
            for j in range(1, G)
        ]

    def regroup(which):
        for q in range(K):
            h, w = q // (K // 2), q % (K // 2)
            span = slice(w * 16, w * 16 + 16)
            a = zrecv[which, 4 * q : 4 * q + 4, 0:A, :].reshape(4 * A, 128)
            ysend[which, :, h, span, :] = dot(mix_a, a, 1, 0).astype(BF).reshape(G, 16, 128)
            b = dot(mix_b, zrecv[which, 4 * q : 4 * q + 4, A : A + B, :].reshape(4 * B, 128), 1, 0)
            turned = pltpu.roll(b, FB, 1)
            for c in range(2):
                piece = (b if c == h else turned)[:, h * FB : (h + 1) * FB]
                ysend[which, c * C : (c + 1) * C, 2, span, h * FB : (h + 1) * FB] = (
                    piece.astype(BF).reshape(C, 16, FB)
                )
        start(y_copies(which))
        yrecv[which, :, g] = ysend[which, g]

    @functools.cache
    def x_near(which):
        own = xall.at[which, r]
        return [
            remote(own, own, x_send.at[which, 0], x_recv.at[which, 0], {"rep": right_x}),
            remote(own, own, x_send.at[which, 1], x_recv.at[which, 1], {"rep": left_x}),
        ]

    @functools.cache
    def x_relay(which):
        top = xall.at[which, left_x, pl.ds(0, HF)]
        low = xall.at[which, right_x, pl.ds(HF, HF)]
        return [
            remote(top, top, x_send.at[which, 2], x_recv.at[which, 2], {"rep": right_x}),
            remote(low, low, x_send.at[which, 3], x_recv.at[which, 3], {"rep": left_x}),
        ]

    def unpack(which):
        rows_of = G * Q
        arrived(y_copies(which))
        for h in range(2):
            xall[which, r, 0:128, h * rows_of : (h + 1) * rows_of] = (
                yrecv[which, h].reshape(rows_of, 128).T
            )
        low = yrecv[which, 2].reshape(rows_of, 128).T
        for h in range(2):
            xall[which, r, 128:F, h * rows_of : (h + 1) * rows_of] = low[h * FB : (h + 1) * FB]
        start(x_near(which))

    def relay(which):
        near, passed = x_near(which), x_relay(which)
        for i in range(2):
            near[i].wait_recv()
            start([passed[i]])

    w_out_t[...] = w_out[...].T
    bias = jnp.broadcast_to(b_in[...], (128, H)).T
    out_bias = jnp.broadcast_to(b_out[...], (128, F)).T

    def widen(column):
        return jnp.concatenate([column] * (S // 128), axis=1) if S >= 128 else column[:, :S]

    @functools.cache
    def half_copies(way):
        return [
            remote(xhalf.at[way, 0], rhalf.at[way, 0], r_send.at[way, 0], r_recv.at[way, 0], {"rep": left_x}),
            remote(xhalf.at[way, 1], rhalf.at[way, 1], r_send.at[way, 1], r_recv.at[way, 1], {"rep": right_x}),
        ]

    @functools.cache
    def full_copies(way):
        return [
            remote(xfull.at[way, 0], rfull.at[way, 0], r_send.at[way, 2], r_recv.at[way, 2], {"rep": left_x}),
            remote(xfull.at[way, 1], rfull.at[way, 1], r_send.at[way, 3], r_recv.at[way, 3], {"rep": right_x}),
        ]

    def partial(way, target):
        span = pl.ds(pl.multiple_of(target * F, F), F)
        return dot(w_out_t[span, :], hid[...], 1, 0) if way == 0 else dot(w_in[span, :], d_pre[...], 1, 0)

    def scatter_start(way):
        far = partial(way, far_x).astype(BF)
        xhalf[way, 0] = far[0:HF]
        xhalf[way, 1] = far[HF:F]
        start(half_copies(way))

    def scatter_middle(way):
        for i, target in ((0, left_x), (1, right_x)):
            mine = partial(way, target)
            half_copies(way)[i].wait_recv()
            came = rhalf[way, i].astype(F32)
            if i == 0:
                xfull[way, i] = jnp.concatenate([mine[0:HF] + came, mine[HF:F]], axis=0).astype(BF)
            else:
                xfull[way, i] = jnp.concatenate([mine[0:HF], mine[HF:F] + came], axis=0).astype(BF)
            start([full_copies(way)[i]])

    @functools.cache
    def b_copies(way):
        return [
            remote(
                back.at[way, lax.rem(g + j, G)], yret.at[way, :, g],
                b_send.at[way, j - 1], b_recv.at[way, j - 1], {"grp": lax.rem(g + j, G)},
            )
            for j in range(1, G)
        ]

    def scatter_end(way):
        rows_of = G * Q
        total = partial(way, r)
        if way == 0:
            total = total + widen(out_bias)
        for i, copy in enumerate(full_copies(way)):
            copy.wait_recv()
            total = total + rfull[way, i].astype(F32)
        value = total.astype(BF)
        low = jnp.concatenate([value[128:F, h * rows_of : (h + 1) * rows_of] for h in range(2)], axis=0)
        pieces = [value[0:128, h * rows_of : (h + 1) * rows_of] for h in range(2)] + [low]
        for i, piece in enumerate(pieces):
            back[way, :, i] = piece.T.reshape(G, Q, 128)
        start(b_copies(way))
        yret[way, :, g] = back[way, g]

    @functools.cache
    def s_copies(way):
        return [
            remote(
                zback.at[way, lax.rem(n + j, N)], zret.at[way, n],
                s_send.at[way, j - 1], s_recv.at[way, j - 1], {"node": lax.rem(n + j, N)},
            )
            for j in order
        ]

    def ungroup(way):
        arrived(b_copies(way))
        for q in range(K):
            h, w = q // (K // 2), q % (K // 2)
            span = slice(w * 16, w * 16 + 16)
            a = yret[way, h, :, span, :].reshape(4 * A, 128)
            zback[way, 4 * q : 4 * q + 4, 0:A, :] = dot(mix_a, a, 0, 0).astype(BF).reshape(4, A, 128)
            b = yret[way, 2, :, span, :].reshape(4 * A, 128)
            for c in range(2):
                part = dot(mix_b, b[c * 4 * B : (c + 1) * 4 * B], 0, 0)
                if c != h:
                    part = pltpu.roll(part, FB, 1)
                zback[way, 4 * q : 4 * q + 4, A : A + B, c * FB : (c + 1) * FB] = (
                    part[:, c * FB : (c + 1) * FB].astype(BF).reshape(4, B, FB)
                )
        start(s_copies(way))
        zret[way, n] = zback[way, n]

    def landed(way):
        arrived(s_copies(way))
        hot = place[...] if way == 0 else place[:, 0:T] + place[:, T : 2 * T]
        a = zret[way, :, 0:A, :].reshape(N * A, 128)
        b = zret[way, :, A : A + B, :].reshape(N * B, 128)
        top = dot(a, hot, 0, 0)
        hot = hot.reshape(N, 2, B, hot.shape[1])
        low = [dot(b, hot[:, c].reshape(N * B, hot.shape[3]), 0, 0)[c * FB : (c + 1) * FB] for c in range(2)]
        return jnp.concatenate([top, low[0] + low[1]], axis=0)

    arrived(z_copies(0))
    regroup(0)
    unpack(0)
    relay(0)
    arrived(z_copies(1))
    regroup(1)
    arrived(x_relay(0))
    acc = dot(w_in[...], xall[0].reshape(D, S), 0, 0) + widen(bias)
    t = jnp.tanh(ROOT * (acc + 0.044715 * acc * acc * acc))
    hid[...] = (0.5 * acc * (1.0 + t)).astype(BF)
    dgelu[...] = 0.5 * (1.0 + t) + 0.5 * acc * (1.0 - t * t) * (ROOT * (1.0 + 3 * 0.044715 * acc * acc))
    unpack(1)
    scatter_start(0)
    relay(1)
    scatter_middle(0)
    arrived(x_relay(1))
    slope = dot(w_out[...], xall[1].reshape(D, S), 1, 0)
    d_pre[...] = (slope * dgelu[...]).astype(BF)
    scatter_start(1)
    scatter_end(0)
    scatter_middle(1)
    ungroup(0)
    scatter_end(1)

    ones = jnp.ones((8, S), BF)
    grad_in[...] = dot(xall[0].reshape(D, S), d_pre[...], 1, 1)
    grad_out[...] = dot(hid[...], xall[1].reshape(D, S), 1, 1)
    outs = [
        pltpu.make_async_copy(grad_in, d_w_in, o_sem.at[0]),
        pltpu.make_async_copy(grad_out, d_w_out, o_sem.at[1]),
    ]
    for copy in outs:
        copy.start()
    d_b_in[...] = dot(ones, d_pre[...], 1, 1)[0:1]
    d_b_out[...] = dot(ones, xall[1, r], 1, 1)[0:1]

    ungroup(1)
    both = landed(0)
    wide = cot[...].astype(F32)
    cut = [both[:, k * T : (k + 1) * T] for k in range(2)]
    mixed[...] = (gates[0:1, :] * cut[0] + gates[1:2, :] * cut[1]).astype(BF)
    sums = [jnp.sum(one * wide, axis=0, keepdims=True) for one in cut]
    sums = jnp.concatenate(sums + [jnp.zeros((6, T), F32)], axis=0)
    dsum[...] = sums
    shares = [
        remote(dsum, drecv.at[j - 1], p_send.at[j - 1], p_recv.at[j - 1], {"rep": lax.rem(r + j, R)})
        for j in range(1, R)
    ]
    start(shares)
    d_tok[...] = landed(1).astype(BF)
    arrived(shares)
    for j in range(R - 1):
        sums = sums + drecv[j]
    d_gates[...] = sums[0:2]
    for copy in outs:
        copy.wait()
    for copy in started:
        copy.wait_send()


def hand_out(*refs):
    count = len(refs) // 3
    sources, results, held = refs[:count], refs[count : 2 * count], refs[2 * count : 3 * count]
    sem_in, sem_out = refs[3 * count :]
    inward = [pltpu.make_async_copy(s, h, sem_in.at[i]) for i, (s, h) in enumerate(zip(sources, held))]
    outward = [pltpu.make_async_copy(h, o, sem_out.at[i]) for i, (h, o) in enumerate(zip(held, results))]
    for copy in inward:
        copy.start()
    for i, copy in enumerate(inward):
        copy.wait()
        outward[i].start()
    for copy in outward:
        copy.wait()


def per_device(tokens, gates, expert_ids, w_in, b_in, w_out, b_out, cotangent):
    N, G, R = lax.axis_size("node"), lax.axis_size("grp"), lax.axis_size("rep")
    T, F = tokens.shape
    _, D, H = w_in.shape
    A, B, Q = G * CAP, G * CAP // 2, 2 * N
    S = 2 * G * Q
    HF = F // 2
    dma = pltpu.SemaphoreType.DMA
    vmem = pl.BlockSpec(memory_space=pltpu.VMEM)
    any_ = pl.BlockSpec(memory_space=pl.ANY)
    shapes = (
        jax.ShapeDtypeStruct((F, T), BF),
        jax.ShapeDtypeStruct((F, T), BF),
        jax.ShapeDtypeStruct((2, T), F32),
        jax.ShapeDtypeStruct((D, H), F32),
        jax.ShapeDtypeStruct((1, H), F32),
        jax.ShapeDtypeStruct((H, D), F32),
        jax.ShapeDtypeStruct((1, F), F32),
    )
    out = pl.pallas_call(
        functools.partial(fused, N, G, R),
        out_shape=shapes,
        in_specs=[vmem] * 8,
        out_specs=(vmem, vmem, vmem, any_, vmem, any_, vmem),
        scratch_shapes=[
            pltpu.VMEM((2, N, A + B, 128), BF),
            pltpu.VMEM((2, N, A + B, 128), BF),
            pltpu.VMEM((N * A, 2 * T), BF),
            pltpu.VMEM((2, G, 3, Q, 128), BF),
            pltpu.VMEM((2, 3, G, Q, 128), BF),
            pltpu.VMEM((2, R, F, S), BF),
            pltpu.VMEM((D, H), BF),
            pltpu.VMEM((H, S), F32),
            pltpu.VMEM((H, S), BF),
            pltpu.VMEM((H, S), BF),
            pltpu.VMEM((2, 2, HF, S), BF),
            pltpu.VMEM((2, 2, F, S), BF),
            pltpu.VMEM((2, 2, HF, S), BF),
            pltpu.VMEM((2, 2, F, S), BF),
            pltpu.VMEM((2, G, 3, Q, 128), BF),
            pltpu.VMEM((2, 3, G, Q, 128), BF),
            pltpu.VMEM((2, N, A + B, 128), BF),
            pltpu.VMEM((2, N, A + B, 128), BF),
            pltpu.VMEM((D, H), F32),
            pltpu.VMEM((H, D), F32),
            pltpu.VMEM((8, T), F32),
            pltpu.VMEM((R - 1, 8, T), F32),
            dma((2, N - 1)),
            dma((2, N - 1)),
            dma((2, G - 1)),
            dma((2, G - 1)),
            dma((2, 4)),
            dma((2, 4)),
            dma((2, 4)),
            dma((2, 4)),
            dma((2, G - 1)),
            dma((2, G - 1)),
            dma((2, N - 1)),
            dma((2, N - 1)),
            dma((R - 1,)),
            dma((R - 1,)),
            dma((2,)),
        ],
        compiler_params=pltpu.CompilerParams(
            collective_id=0, has_side_effects=True, vmem_limit_bytes=60 * 2**20
        ),
    )(
        tokens.T, cotangent.T, expert_ids.T, gates.T,
        w_in[0], b_in, w_out[0], b_out,
    )
    out = pl.pallas_call(
        hand_out,
        out_shape=shapes,
        in_specs=[any_] * 7,
        out_specs=(any_,) * 7,
        scratch_shapes=[pltpu.VMEM(one.shape, one.dtype) for one in shapes] + [dma((7,)), dma((7,))],
    )(*out)
    mixed, d_tok, d_gates, d_w_in, d_b_in, d_w_out, d_b_out = out
    return (mixed.T, d_tok.T, d_gates.T, d_w_in[None], d_b_in, d_w_out[None], d_b_out)


def solution(mesh):
    both = ("node", "grp")
    return jax.shard_map(
        per_device,
        mesh=mesh,
        in_specs=(
            P(both, "rep"),
            P(both, None),
            P(both, None),
            P(both, None, "rep"),
            P(both, "rep"),
            P(both, "rep", None),
            P(both, "rep"),
            P(both, "rep"),
        ),
        out_specs=(
            P(both, "rep"),
            P(both, "rep"),
            P(both, None),
            P(both, None, "rep"),
            P(both, "rep"),
            P(both, "rep", None),
            P(both, "rep"),
        ),
        check_vma=False,
    )
```

```python
import functools
import math

import jax
import jax.numpy as jnp
from jax import lax
from jax.experimental import pallas as pl
from jax.experimental.pallas import tpu as pltpu
from jax.sharding import PartitionSpec as P

MESH = pl.DeviceIdType.MESH
CAP = 4
BF = jnp.bfloat16
F32 = jnp.float32
ROOT = math.sqrt(2.0 / math.pi)


def dot(a, b, ca, cb):
    return lax.dot_general(a, b, (((ca,), (cb,)), ((), ())), preferred_element_type=F32)


def fused(
    N, G, R,
    tok, cot, ids, gates, w_in_hbm, b_in, w_out_hbm, b_out,
    mixed, d_tok, d_gates, d_w_in, d_b_in, d_w_out, d_b_out,
    place, ysend, yrecv, zsend, zrecv, xall, w_in, w_out, w_out_t, dgelu, hid, d_pre,
    xhalf, xfull, rhalf, rfull, zback, zret, back, yret, grad_in, grad_out, dsum, drecv,
    y_send, y_recv, z_send, z_recv, x_send, x_recv, r_send, r_recv,
    s_send, s_recv, b_send, b_recv, p_send, p_recv, o_sem, reach,
):
    n, g, r = lax.axis_index("node"), lax.axis_index("grp"), lax.axis_index("rep")
    F, T = tok.shape
    D, H = w_in.shape
    A = G * CAP
    B = A // 2
    K = N // 4
    M = N // 2
    Q = 2 * N
    W = M * B
    HF, FB = F // 2, F - 128
    C = G // 2

    right_x, left_x = lax.rem(r + 1, R), lax.rem(r + R - 1, R)
    far_x = lax.rem(r + 2, R)

    barrier = pltpu.get_barrier_semaphore()
    peers = [{"node": lax.rem(n + j, N)} for j in (1, N - 1)]
    peers += [{"grp": lax.rem(g + j, G)} for j in range(1, G)]
    peers += [{"rep": lax.rem(r + j, R)} for j in range(1, R)]
    for peer in peers:
        pl.semaphore_signal(barrier, inc=1, device_id=peer, device_id_type=MESH)

    weights = [
        pltpu.make_async_copy(w_in_hbm, w_in, o_sem.at[2]),
        pltpu.make_async_copy(w_out_hbm, w_out, o_sem.at[3]),
    ]
    for copy in weights:
        copy.start()

    def remote(src, dst, send, recv, peer):
        return pltpu.make_async_remote_copy(
            src_ref=src, dst_ref=dst, send_sem=send, recv_sem=recv,
            device_id=peer, device_id_type=MESH,
        )

    started = []

    def start(copies):
        for copy in copies:
            copy.start()
        started.extend(copies)

    def arrived(copies):
        for copy in copies:
            copy.wait_recv()

    ids_i = ids[...]
    ids_f = ids_i.astype(F32)
    rows = [ids_f[k : k + 1, :] for k in range(2)]
    ahead = lax.rem(lax.div(ids_i, G) - n + N, N)
    base = (lax.rem(ids_i, G) * N + ahead) * CAP
    base = jnp.where(ids_i < N * G, base, -CAP * T).astype(F32)
    cols = [jnp.broadcast_to(row, (T, T)).T for row in rows]
    earlier = lax.broadcasted_iota(jnp.int32, (T, T), 0) < lax.broadcasted_iota(jnp.int32, (T, T), 1)
    slot = lax.broadcasted_iota(jnp.int32, (N * A, T), 0).astype(F32)
    for k in range(2):
        same = jnp.where(cols[0] == rows[k], 1.0, 0.0) + jnp.where(cols[1] == rows[k], 1.0, 0.0)
        rank = jnp.sum(jnp.where(earlier, same, 0.0), axis=0, keepdims=True)
        target = base[k : k + 1, :] + rank
        place[:, k * T : (k + 1) * T] = jnp.where(slot == target, 1.0, 0.0).astype(BF)

    @functools.cache
    def y_copies(which):
        return [
            remote(
                ysend.at[which, lax.rem(g + j, G)], yrecv.at[which, :, g],
                y_send.at[which, j - 1], y_recv.at[which, j - 1], {"grp": lax.rem(g + j, G)},
            )
            for j in range(1, G)
        ]

    def lay(which):
        if which == 0:
            got = dot(place[:, 0:T] + place[:, T : 2 * T], tok[...], 1, 1)
        else:
            wide = cot[...].astype(F32)
            grads = [(gates[k : k + 1, :] * wide).astype(BF) for k in range(2)]
            got = dot(place[...], jnp.concatenate(grads, axis=1), 1, 1)
        got = got.reshape(G, 2, Q, F)
        for h in range(2):
            ysend[which, :, h] = got[:, h, :, 0:128].astype(BF)
            ysend[which, :, 2, :, h * FB : (h + 1) * FB] = got[:, h, :, 128:F].astype(BF)

    def shuffle(groups):
        size = 4 * groups * CAP
        i = lax.broadcasted_iota(jnp.int32, (size, size), 0)
        j = lax.broadcasted_iota(jnp.int32, (size, size), 1)
        e, v, c = i // (4 * CAP), lax.rem(i // CAP, 4), lax.rem(i, CAP)
        return jnp.where(j == (v * groups + e) * CAP + c, 1.0, 0.0).astype(BF)

    def y_to_z(source, target):
        for q in range(K):
            h, w = q // (K // 2), q % (K // 2)
            span = slice(w * 16, w * 16 + 16)
            a = source[h, :, span, :].reshape(4 * A, 128)
            target[4 * q : 4 * q + 4, 0:A, :] = dot(mix_a, a, 0, 0).astype(BF).reshape(4, A, 128)
            b = source[2, :, span, :].reshape(4 * A, 128)
            for c in range(2):
                part = dot(mix_b, b[c * 4 * B : (c + 1) * 4 * B], 0, 0)
                if c != h:
                    part = pltpu.roll(part, FB, 1)
                target[4 * q : 4 * q + 4, A : A + B, c * FB : (c + 1) * FB] = (
                    part[:, c * FB : (c + 1) * FB].astype(BF).reshape(4, B, FB)
                )

    def z_to_y(source, target):
        for q in range(K):
            h, w = q // (K // 2), q % (K // 2)
            span = slice(w * 16, w * 16 + 16)
            a = source[4 * q : 4 * q + 4, 0:A, :].reshape(4 * A, 128)
            target[:, h, span, :] = dot(mix_a, a, 1, 0).astype(BF).reshape(G, 16, 128)
            b = dot(mix_b, source[4 * q : 4 * q + 4, A : A + B, :].reshape(4 * B, 128), 1, 0)
            turned = pltpu.roll(b, FB, 1)
            for c in range(2):
                piece = (b if c == h else turned)[:, h * FB : (h + 1) * FB]
                target[c * C : (c + 1) * C, 2, span, h * FB : (h + 1) * FB] = (
                    piece.astype(BF).reshape(C, 16, FB)
                )

    near_first = [0]
    for j in range(1, M):
        near_first += [j, N - j]
    near_first.append(M)
    spot = {j: i for i, j in enumerate(near_first)}

    @functools.cache
    def z_copies(which, part):
        return [
            remote(
                zsend.at[which, N - j], zrecv.at[which, spot[j]],
                z_send.at[which, j - 1], z_recv.at[which, j - 1], {"node": lax.rem(n + N - j, N)},
            )
            for j in near_first[part * M : (part + 1) * M]
            if j
        ]

    @functools.cache
    def x_copies(which, part, stage):
        own = xall.at[which, part, r]
        top, low = own.at[pl.ds(0, HF)], own.at[pl.ds(HF, HF)]
        if stage == 0:
            pair = top, low
        elif stage == 1:
            pair = low, top
        else:
            pair = (
                xall.at[which, part, left_x, pl.ds(0, HF)],
                xall.at[which, part, right_x, pl.ds(HF, HF)],
            )
        return [
            remote(
                ref, ref, x_send.at[which, part, stage, i], x_recv.at[which, part, stage, i],
                {"rep": (right_x, left_x)[i]},
            )
            for i, ref in enumerate(pair)
        ]

    def unpack(which, part):
        arrived(z_copies(which, part))
        nodes = slice(part * M, (part + 1) * M)
        low = zrecv[which, nodes, A : A + B, :].reshape(W, 128).T
        for c in range(2):
            lanes = slice(c * W, (c + 1) * W)
            a = zrecv[which, nodes, c * B : (c + 1) * B, :].reshape(W, 128)
            xall[which, part, r, 0:128, lanes] = a.T
            xall[which, part, r, 128:F, lanes] = low[c * FB : (c + 1) * FB]
        start(x_copies(which, part, 0))
        start(x_copies(which, part, 1))

    def relay(which, part):
        for i in range(2):
            x_copies(which, part, 0)[i].wait_recv()
            start([x_copies(which, part, 2)[i]])

    def gathered(which, part):
        arrived(x_copies(which, part, 1))
        arrived(x_copies(which, part, 2))
        return xall[which, part].reshape(D, 2 * W)

    def widen(column, width):
        return jnp.concatenate([column] * (width // 128), axis=1) if width >= 128 else column[:, :width]

    @functools.cache
    def r_copies(way, part, stage):
        found = []
        for i in range(2):
            peer = {"rep": (left_x, right_x)[i]}
            if stage == 0:
                src, dst = xhalf.at[way, part, i], rhalf.at[way, part, i]
            else:
                span = pl.ds(HF if (i == 0) == (stage == 1) else 0, HF)
                src, dst = xfull.at[way, part, i, span], rfull.at[way, part, i, span]
            found.append(
                remote(src, dst, r_send.at[way, part, stage, i], r_recv.at[way, part, stage, i], peer)
            )
        return found

    def partial(way, part, target):
        span = pl.ds(pl.multiple_of(target * F, F), F)
        if way == 0:
            return dot(w_out_t[span, :], hid[part], 1, 0)
        return dot(w_in[span, :], d_pre[part], 1, 0)

    def sums_start(way, part):
        far = partial(way, part, far_x).astype(BF)
        xhalf[way, part, 0] = far[0:HF]
        xhalf[way, part, 1] = far[HF:F]
        start(r_copies(way, part, 0))
        for i, target in ((0, left_x), (1, right_x)):
            xfull[way, part, i] = partial(way, part, target).astype(BF)
            start([r_copies(way, part, 1)[i]])

    def sums_middle(way, part):
        for i in range(2):
            r_copies(way, part, 0)[i].wait_recv()
            span = slice(0, HF) if i == 0 else slice(HF, F)
            total = xfull[way, part, i, span].astype(F32) + rhalf[way, part, i].astype(F32)
            xfull[way, part, i, span] = total.astype(BF)
            start([r_copies(way, part, 2)[i]])

    @functools.cache
    def s_copies(way, part):
        return [
            remote(
                zback.at[way, spot[j]], zret.at[way, N - j],
                s_send.at[way, j - 1], s_recv.at[way, j - 1], {"node": lax.rem(n + j, N)},
            )
            for j in near_first[part * M : (part + 1) * M]
            if j
        ]

    def sums_end(way, part):
        total = partial(way, part, r)
        if way == 0:
            total = total + widen(out_bias, 2 * W)
        for i in range(2):
            r_copies(way, part, 1)[i].wait_recv()
            r_copies(way, part, 2)[i].wait_recv()
            total = total + rfull[way, part, i].astype(F32)
        value = total.astype(BF)
        nodes = slice(part * M, (part + 1) * M)
        low = jnp.concatenate([value[128:F, 0:W], value[128:F, W : 2 * W]], axis=0)
        zback[way, nodes, A : A + B, :] = low.T.reshape(M, B, 128)
        for c in range(2):
            zback[way, nodes, c * B : (c + 1) * B, :] = (
                value[0:128, c * W : (c + 1) * W].T.reshape(M, B, 128)
            )
        start(s_copies(way, part))
        if part == 0:
            zret[way, 0] = zback[way, 0]

    @functools.cache
    def b_copies(way):
        return [
            remote(
                back.at[way, lax.rem(g + j, G)], yret.at[way, :, g],
                b_send.at[way, j - 1], b_recv.at[way, j - 1], {"grp": lax.rem(g + j, G)},
            )
            for j in range(1, G)
        ]

    def homeward(way):
        for part in range(2):
            arrived(s_copies(way, part))
        z_to_y(zret.at[way], back.at[way])
        start(b_copies(way))
        yret[way, :, g] = back[way, g]

    def landed(way):
        arrived(b_copies(way))
        hot = place[...] if way == 0 else place[:, 0:T] + place[:, T : 2 * T]
        width = hot.shape[1]
        hot = hot.reshape(G, 2, Q, width)
        low = yret[way, 2].reshape(G * Q, 128)
        top, rest = 0.0, 0.0
        for h in range(2):
            one = hot[:, h].reshape(G * Q, width)
            top += dot(yret[way, h].reshape(G * Q, 128), one, 0, 0)
            rest += dot(low, one, 0, 0)[h * FB : (h + 1) * FB]
        return jnp.concatenate([top, rest], axis=0)

    def forward(part):
        x = gathered(0, part)
        acc = dot(w_in[...], x, 0, 0) + widen(bias, 2 * W)
        t = jnp.tanh(ROOT * (acc + 0.044715 * acc * acc * acc))
        hid[part] = (0.5 * acc * (1.0 + t)).astype(BF)
        dgelu[part] = 0.5 * (1.0 + t) + 0.5 * acc * (1.0 - t * t) * (
            ROOT * (1.0 + 3 * 0.044715 * acc * acc)
        )

    def backward(part):
        slope = dot(w_out[...], gathered(1, part), 1, 0)
        d_pre[part] = (slope * dgelu[part]).astype(BF)

    lay(0)
    pl.semaphore_wait(barrier, len(peers))
    start(y_copies(0))
    yrecv[0, :, g] = ysend[0, g]
    lay(1)
    start(y_copies(1))
    yrecv[1, :, g] = ysend[1, g]
    far, level = 1, 0
    while far < M:
        for j in (far, N - far):
            pl.semaphore_signal(
                reach.at[level], inc=1, device_id={"node": lax.rem(n + j, N)}, device_id_type=MESH
            )
        pl.semaphore_wait(reach.at[level], 2)
        far, level = 2 * far, level + 1
    mix_a, mix_b = shuffle(G), shuffle(C)
    for which in range(2):
        arrived(y_copies(which))
        y_to_z(yrecv.at[which], zsend.at[which])
        start(z_copies(which, 0))
        start(z_copies(which, 1))
        zrecv[which, 0] = zsend[which, 0]
    for copy in weights:
        copy.wait()
    w_out_t[...] = w_out[...].T
    bias = jnp.broadcast_to(b_in[...], (128, H)).T
    out_bias = jnp.broadcast_to(b_out[...], (128, F)).T

    unpack(0, 0)
    relay(0, 0)
    unpack(0, 1)
    relay(0, 1)
    forward(0)
    unpack(1, 0)
    sums_start(0, 0)
    forward(1)
    relay(1, 0)
    sums_middle(0, 0)
    sums_start(0, 1)
    unpack(1, 1)
    backward(0)
    sums_start(1, 0)
    relay(1, 1)
    sums_middle(0, 1)
    sums_end(0, 0)
    sums_middle(1, 0)
    backward(1)
    sums_start(1, 1)
    sums_end(0, 1)
    sums_end(1, 0)
    sums_middle(1, 1)

    ones = jnp.ones((8, 2 * W), BF)
    grad_in[...] = sum(dot(xall[0, part].reshape(D, 2 * W), d_pre[part], 1, 1) for part in range(2))
    outs = [
        pltpu.make_async_copy(grad_in, d_w_in, o_sem.at[0]),
        pltpu.make_async_copy(grad_out, d_w_out, o_sem.at[1]),
    ]
    outs[0].start()
    sums_end(1, 1)
    grad_out[...] = sum(dot(hid[part], xall[1, part].reshape(D, 2 * W), 1, 1) for part in range(2))
    outs[1].start()
    d_b_in[...] = sum(dot(ones, d_pre[part], 1, 1) for part in range(2))[0:1]
    d_b_out[...] = sum(dot(ones, xall[1, part, r], 1, 1) for part in range(2))[0:1]

    homeward(0)
    both = landed(0)
    wide = cot[...].astype(F32)
    cut = [both[:, k * T : (k + 1) * T] for k in range(2)]
    mixed[...] = (gates[0:1, :] * cut[0] + gates[1:2, :] * cut[1]).astype(BF)
    sums = [jnp.sum(one * wide, axis=0, keepdims=True) for one in cut]
    sums = jnp.concatenate(sums + [jnp.zeros((6, T), F32)], axis=0)
    dsum[...] = sums
    shares = [
        remote(dsum, drecv.at[j - 1], p_send.at[j - 1], p_recv.at[j - 1], {"rep": lax.rem(r + j, R)})
        for j in range(1, R)
    ]
    start(shares)
    homeward(1)
    arrived(shares)
    for j in range(R - 1):
        sums = sums + drecv[j]
    d_gates[...] = sums[0:2]
    d_tok[...] = landed(1).astype(BF)
    for copy in outs:
        copy.wait()
    for copy in started:
        copy.wait_send()


def hand_out(*refs):
    count = len(refs) // 3
    sources, results, held = refs[:count], refs[count : 2 * count], refs[2 * count : 3 * count]
    sem_in, sem_out = refs[3 * count :]
    inward = [pltpu.make_async_copy(s, h, sem_in.at[i]) for i, (s, h) in enumerate(zip(sources, held))]
    outward = [pltpu.make_async_copy(h, o, sem_out.at[i]) for i, (h, o) in enumerate(zip(held, results))]
    for copy in inward:
        copy.start()
    for i, copy in enumerate(inward):
        copy.wait()
        outward[i].start()
    for copy in outward:
        copy.wait()


def per_device(tokens, gates, expert_ids, w_in, b_in, w_out, b_out, cotangent):
    N, G, R = lax.axis_size("node"), lax.axis_size("grp"), lax.axis_size("rep")
    T, F = tokens.shape
    _, D, H = w_in.shape
    A, B, Q = G * CAP, G * CAP // 2, 2 * N
    W = N // 2 * B
    HF = F // 2
    dma = pltpu.SemaphoreType.DMA
    vmem = pl.BlockSpec(memory_space=pltpu.VMEM)
    any_ = pl.BlockSpec(memory_space=pl.ANY)
    shapes = (
        jax.ShapeDtypeStruct((F, T), BF),
        jax.ShapeDtypeStruct((F, T), BF),
        jax.ShapeDtypeStruct((2, T), F32),
        jax.ShapeDtypeStruct((D, H), F32),
        jax.ShapeDtypeStruct((1, H), F32),
        jax.ShapeDtypeStruct((H, D), F32),
        jax.ShapeDtypeStruct((1, F), F32),
    )
    out = pl.pallas_call(
        functools.partial(fused, N, G, R),
        out_shape=shapes,
        in_specs=[vmem, vmem, vmem, vmem, any_, vmem, any_, vmem],
        out_specs=(vmem, vmem, vmem, any_, vmem, any_, vmem),
        scratch_shapes=[
            pltpu.VMEM((N * A, 2 * T), BF),
            pltpu.VMEM((2, G, 3, Q, 128), BF),
            pltpu.VMEM((2, 3, G, Q, 128), BF),
            pltpu.VMEM((2, N, A + B, 128), BF),
            pltpu.VMEM((2, N, A + B, 128), BF),
            pltpu.VMEM((2, 2, R, F, 2 * W), BF),
            pltpu.VMEM((D, H), BF),
            pltpu.VMEM((H, D), BF),
            pltpu.VMEM((D, H), BF),
            pltpu.VMEM((2, H, 2 * W), F32),
            pltpu.VMEM((2, H, 2 * W), BF),
            pltpu.VMEM((2, H, 2 * W), BF),
            pltpu.VMEM((2, 2, 2, HF, 2 * W), BF),
            pltpu.VMEM((2, 2, 2, F, 2 * W), BF),
            pltpu.VMEM((2, 2, 2, HF, 2 * W), BF),
            pltpu.VMEM((2, 2, 2, F, 2 * W), BF),
            pltpu.VMEM((2, N, A + B, 128), BF),
            pltpu.VMEM((2, N, A + B, 128), BF),
            pltpu.VMEM((2, G, 3, Q, 128), BF),
            pltpu.VMEM((2, 3, G, Q, 128), BF),
            pltpu.VMEM((D, H), F32),
            pltpu.VMEM((H, D), F32),
            pltpu.VMEM((8, T), F32),
            pltpu.VMEM((R - 1, 8, T), F32),
            dma((2, G - 1)),
            dma((2, G - 1)),
            dma((2, N - 1)),
            dma((2, N - 1)),
            dma((2, 2, 3, 2)),
            dma((2, 2, 3, 2)),
            dma((2, 2, 3, 2)),
            dma((2, 2, 3, 2)),
            dma((2, N - 1)),
            dma((2, N - 1)),
            dma((2, G - 1)),
            dma((2, G - 1)),
            dma((R - 1,)),
            dma((R - 1,)),
            dma((4,)),
            pltpu.SemaphoreType.REGULAR((4,)),
        ],
        compiler_params=pltpu.CompilerParams(
            collective_id=0, has_side_effects=True, vmem_limit_bytes=60 * 2**20
        ),
    )(
        tokens.T, cotangent.T, expert_ids.T, gates.T,
        w_in[0], b_in, w_out[0], b_out,
    )
    out = pl.pallas_call(
        hand_out,
        out_shape=shapes,
        in_specs=[any_] * 7,
        out_specs=(any_,) * 7,
        scratch_shapes=[pltpu.VMEM(one.shape, one.dtype) for one in shapes] + [dma((7,)), dma((7,))],
    )(*out)
    mixed, d_tok, d_gates, d_w_in, d_b_in, d_w_out, d_b_out = out
    return (mixed.T, d_tok.T, d_gates.T, d_w_in[None], d_b_in, d_w_out[None], d_b_out)


def solution(mesh):
    both = ("node", "grp")
    return jax.shard_map(
        per_device,
        mesh=mesh,
        in_specs=(
            P(both, "rep"),
            P(both, None),
            P(both, None),
            P(both, None, "rep"),
            P(both, "rep"),
            P(both, "rep", None),
            P(both, "rep"),
            P(both, "rep"),
        ),
        out_specs=(
            P(both, "rep"),
            P(both, "rep"),
            P(both, None),
            P(both, None, "rep"),
            P(both, "rep"),
            P(both, "rep", None),
            P(both, "rep"),
        ),
        check_vma=False,
    )
```

```python
import functools
import math

import jax
import jax.numpy as jnp
from jax import lax
from jax.experimental import pallas as pl
from jax.experimental.pallas import tpu as pltpu
from jax.sharding import PartitionSpec as P

MESH = pl.DeviceIdType.MESH
CAP = 4
VLIM = 60
BF = jnp.bfloat16
F32 = jnp.float32
ROOT = math.sqrt(2.0 / math.pi)


def dot(a, b, ca, cb):
    return lax.dot_general(a, b, (((ca,), (cb,)), ((), ())), preferred_element_type=F32)


def fused(
    N, G, R,
    tok, cot, ids, gates, w_in_hbm, b_in, w_out_hbm, b_out,
    mixed, d_tok, d_gates, d_w_in, d_b_in, d_w_out, d_b_out,
    place, ysend, yrecv, zsend, zrecv, xall, w_in, w_out, w_out_t, dgelu, hid, d_pre,
    xhalf, xfull, rhalf, rfull, zback, zret, back, yret, grad_in, grad_out, dsum, drecv,
    y_send, y_recv, z_send, z_recv, x_send, x_recv, r_send, r_recv,
    s_send, s_recv, b_send, b_recv, p_send, p_recv, o_sem, reach,
):
    n, g, r = lax.axis_index("node"), lax.axis_index("grp"), lax.axis_index("rep")
    F, T = tok.shape
    D, H = w_in.shape
    A = G * CAP
    B = A // 2
    K = N // 4
    M = N // 2
    Q = 2 * N
    W = M * B
    HF, FB = F // 2, F - 128
    C = G // 2

    right_x, left_x = lax.rem(r + 1, R), lax.rem(r + R - 1, R)
    far_x = lax.rem(r + 2, R)

    barrier = pltpu.get_barrier_semaphore()
    peers = [{"node": lax.rem(n + j, N)} for j in (1, N - 1)]
    peers += [{"grp": lax.rem(g + j, G)} for j in range(1, G)]
    peers += [{"rep": lax.rem(r + j, R)} for j in range(1, R)]
    for peer in peers:
        pl.semaphore_signal(barrier, inc=1, device_id=peer, device_id_type=MESH)

    weights = [
        pltpu.make_async_copy(w_in_hbm, w_in, o_sem.at[2]),
        pltpu.make_async_copy(w_out_hbm, w_out, o_sem.at[3]),
    ]
    for copy in weights:
        copy.start()

    def remote(src, dst, send, recv, peer):
        return pltpu.make_async_remote_copy(
            src_ref=src, dst_ref=dst, send_sem=send, recv_sem=recv,
            device_id=peer, device_id_type=MESH,
        )

    started = []

    def start(copies):
        for copy in copies:
            copy.start()
        started.extend(copies)

    def arrived(copies):
        for copy in copies:
            copy.wait_recv()

    ids_i = ids[...]
    ids_f = ids_i.astype(F32)
    rows = [ids_f[k : k + 1, :] for k in range(2)]
    near_first = [0]
    for j in range(1, M):
        near_first += [j, N - j]
    near_first.append(M)
    spot = {j: i for i, j in enumerate(near_first)}
    away = lax.rem(n + 16 * N - lax.div(ids_i, G), N)
    ahead = sum(jnp.where(away == j, spot[j], 0) for j in range(1, N))
    base = (lax.rem(ids_i, G) * N + ahead) * CAP
    base = jnp.where(ids_i < N * G, base, -CAP * T).astype(F32)
    cols = [jnp.broadcast_to(row, (T, T)).T for row in rows]
    earlier = lax.broadcasted_iota(jnp.int32, (T, T), 0) < lax.broadcasted_iota(jnp.int32, (T, T), 1)
    slot = lax.broadcasted_iota(jnp.int32, (N * A, T), 0).astype(F32)
    for k in range(2):
        same = jnp.where(cols[0] == rows[k], 1.0, 0.0) + jnp.where(cols[1] == rows[k], 1.0, 0.0)
        rank = jnp.sum(jnp.where(earlier, same, 0.0), axis=0, keepdims=True)
        target = base[k : k + 1, :] + rank
        place[:, k * T : (k + 1) * T] = jnp.where(slot == target, 1.0, 0.0).astype(BF)

    @functools.cache
    def y_copies(which, part):
        return [
            remote(
                ysend.at[which, part, lax.rem(g + j, G)], yrecv.at[which, part, g],
                y_send.at[which, part, j - 1], y_recv.at[which, part, j - 1], {"grp": lax.rem(g + j, G)},
            )
            for j in range(1, G)
        ]

    def lay(which):
        if which == 0:
            got = dot(place[:, 0:T] + place[:, T : 2 * T], tok[...], 1, 1)
        else:
            wide = cot[...].astype(F32)
            grads = [(gates[k : k + 1, :] * wide).astype(BF) for k in range(2)]
            got = dot(place[...], jnp.concatenate(grads, axis=1), 1, 1)
        got = got.reshape(G, 2, Q, F)
        for h in range(2):
            ysend[which, h, :, 0:Q] = got[:, h, :, 0:128].astype(BF)
            for w in range(K // 2):
                ysend[which, h, :, Q : Q + 16, w * FB : (w + 1) * FB] = (
                    got[:, h, w * 16 : (w + 1) * 16, 128:F].astype(BF)
                )

    def y_start(which, part):
        start(y_copies(which, part))
        yrecv[which, part, g] = ysend[which, part, g]

    def shuffle(groups):
        size = 4 * groups * CAP
        i = lax.broadcasted_iota(jnp.int32, (size, size), 0)
        j = lax.broadcasted_iota(jnp.int32, (size, size), 1)
        e, v, c = i // (4 * CAP), lax.rem(i // CAP, 4), lax.rem(i, CAP)
        return jnp.where(j == (v * groups + e) * CAP + c, 1.0, 0.0).astype(BF)

    def y_to_z(which, part):
        arrived(y_copies(which, part))
        source, target = yrecv.at[which, part], zsend.at[which]
        b = source[:, Q : Q + 16, :].reshape(4 * A, 128)
        for w in range(K // 2):
            q = part * (K // 2) + w
            a = source[:, w * 16 : w * 16 + 16, :].reshape(4 * A, 128)
            target[4 * q : 4 * q + 4, 0:A, :] = dot(mix_a, a, 0, 0).astype(BF).reshape(4, A, 128)
            for c in range(2):
                piece = dot(mix_b, b[c * 4 * B : (c + 1) * 4 * B], 0, 0)
                if c != w:
                    piece = pltpu.roll(piece, FB, 1)
                target[4 * q : 4 * q + 4, A : A + B, c * FB : (c + 1) * FB] = (
                    piece[:, c * FB : (c + 1) * FB].astype(BF).reshape(4, B, FB)
                )
        start(z_copies(which, part))
        if part == 0:
            zrecv[which, 0] = zsend[which, 0]

    def z_to_y(source, target, part):
        for w in range(K // 2):
            q = part * (K // 2) + w
            a = source[4 * q : 4 * q + 4, 0:A, :].reshape(4 * A, 128)
            target[:, w * 16 : w * 16 + 16, :] = dot(mix_a, a, 1, 0).astype(BF).reshape(G, 16, 128)
            b = dot(mix_b, source[4 * q : 4 * q + 4, A : A + B, :].reshape(4 * B, 128), 1, 0)
            turned = pltpu.roll(b, FB, 1)
            for c in range(2):
                piece = (b if c == w else turned)[:, w * FB : (w + 1) * FB]
                target[c * C : (c + 1) * C, Q : Q + 16, w * FB : (w + 1) * FB] = (
                    piece.astype(BF).reshape(C, 16, FB)
                )

    @functools.cache
    def z_copies(which, part):
        return [
            remote(
                zsend.at[which, spot[j]], zrecv.at[which, spot[j]],
                z_send.at[which, j - 1], z_recv.at[which, j - 1], {"node": lax.rem(n + N - j, N)},
            )
            for j in reversed(near_first[part * M : (part + 1) * M])
            if j
        ]

    @functools.cache
    def x_copies(which, part, stage):
        own = xall.at[which, part, r]
        top, low = own.at[pl.ds(0, HF)], own.at[pl.ds(HF, HF)]
        if stage == 0:
            pair = top, low
        elif stage == 1:
            pair = low, top
        else:
            pair = (
                xall.at[which, part, left_x, pl.ds(0, HF)],
                xall.at[which, part, right_x, pl.ds(HF, HF)],
            )
        return [
            remote(
                ref, ref, x_send.at[which, part, stage, i], x_recv.at[which, part, stage, i],
                {"rep": (right_x, left_x)[i]},
            )
            for i, ref in enumerate(pair)
        ]

    def unpack(which, part):
        arrived(z_copies(which, part))
        nodes = slice(part * M, (part + 1) * M)
        low = zrecv[which, nodes, A : A + B, :].reshape(W, 128).T
        for c in range(2):
            lanes = slice(c * W, (c + 1) * W)
            a = zrecv[which, nodes, c * B : (c + 1) * B, :].reshape(W, 128)
            xall[which, part, r, 0:128, lanes] = a.T
            xall[which, part, r, 128:F, lanes] = low[c * FB : (c + 1) * FB]
        start(x_copies(which, part, 0))
        start(x_copies(which, part, 1))

    def relay(which, part):
        for i in range(2):
            x_copies(which, part, 0)[i].wait_recv()
            start([x_copies(which, part, 2)[i]])

    def gathered(which, part):
        arrived(x_copies(which, part, 1))
        arrived(x_copies(which, part, 2))
        return xall[which, part].reshape(D, 2 * W)

    def widen(column, width):
        return jnp.concatenate([column] * (width // 128), axis=1) if width >= 128 else column[:, :width]

    @functools.cache
    def r_copies(way, part, stage):
        found = []
        for i in range(2):
            peer = {"rep": (left_x, right_x)[i]}
            if stage == 0:
                src, dst = xhalf.at[way, part, i], rhalf.at[way, part, i]
            else:
                span = pl.ds(HF if (i == 0) == (stage == 1) else 0, HF)
                src, dst = xfull.at[way, part, i, span], rfull.at[way, part, i, span]
            found.append(
                remote(src, dst, r_send.at[way, part, stage, i], r_recv.at[way, part, stage, i], peer)
            )
        return found

    def partial(way, part, target):
        span = pl.ds(pl.multiple_of(target * F, F), F)
        if way == 0:
            return dot(w_out_t[span, :], hid[part], 1, 0)
        return dot(w_in[span, :], d_pre[part], 1, 0)

    def sums_start(way, part):
        far = partial(way, part, far_x).astype(BF)
        xhalf[way, part, 0] = far[0:HF]
        xhalf[way, part, 1] = far[HF:F]
        start(r_copies(way, part, 0))
        for i, target in ((0, left_x), (1, right_x)):
            xfull[way, part, i] = partial(way, part, target).astype(BF)
            start([r_copies(way, part, 1)[i]])

    def sums_middle(way, part):
        for i in range(2):
            r_copies(way, part, 0)[i].wait_recv()
            span = slice(0, HF) if i == 0 else slice(HF, F)
            total = xfull[way, part, i, span].astype(F32) + rhalf[way, part, i].astype(F32)
            xfull[way, part, i, span] = total.astype(BF)
            start([r_copies(way, part, 2)[i]])

    @functools.cache
    def s_copies(way, part):
        return [
            remote(
                zback.at[way, spot[j]], zret.at[way, spot[j]],
                s_send.at[way, j - 1], s_recv.at[way, j - 1], {"node": lax.rem(n + j, N)},
            )
            for j in reversed(near_first[part * M : (part + 1) * M])
            if j
        ]

    def sums_end(way, part):
        total = partial(way, part, r)
        if way == 0:
            total = total + widen(out_bias, 2 * W)
        for i in range(2):
            r_copies(way, part, 1)[i].wait_recv()
            r_copies(way, part, 2)[i].wait_recv()
            total = total + rfull[way, part, i].astype(F32)
        value = total.astype(BF)
        nodes = slice(part * M, (part + 1) * M)
        low = jnp.concatenate([value[128:F, 0:W], value[128:F, W : 2 * W]], axis=0)
        zback[way, nodes, A : A + B, :] = low.T.reshape(M, B, 128)
        for c in range(2):
            zback[way, nodes, c * B : (c + 1) * B, :] = (
                value[0:128, c * W : (c + 1) * W].T.reshape(M, B, 128)
            )
        start(s_copies(way, part))
        if part == 0:
            zret[way, 0] = zback[way, 0]

    @functools.cache
    def b_copies(way, part):
        return [
            remote(
                back.at[way, part, lax.rem(g + j, G)], yret.at[way, part, g],
                b_send.at[way, part, j - 1], b_recv.at[way, part, j - 1], {"grp": lax.rem(g + j, G)},
            )
            for j in range(1, G)
        ]

    def homeward(way, part):
        arrived(s_copies(way, part))
        z_to_y(zret.at[way], back.at[way, part], part)
        start(b_copies(way, part))
        yret[way, part, g] = back[way, part, g]

    def landed(way):
        hot = place[...] if way == 0 else place[:, 0:T] + place[:, T : 2 * T]
        width = hot.shape[1]
        hot = hot.reshape(G, 2, Q, width)
        top, rest = 0.0, 0.0
        for h in (0, 1):
            arrived(b_copies(way, h))
            top += dot(yret[way, h, :, 0:Q].reshape(G * Q, 128), hot[:, h].reshape(G * Q, width), 0, 0)
            low = yret[way, h, :, Q : Q + 16].reshape(G * 16, 128)
            for w in range(K // 2):
                one = hot[:, h, w * 16 : (w + 1) * 16].reshape(G * 16, width)
                rest += dot(low, one, 0, 0)[w * FB : (w + 1) * FB]
        return jnp.concatenate([top, rest], axis=0)

    def forward(part):
        x = gathered(0, part)
        acc = dot(w_in[...], x, 0, 0) + widen(bias, 2 * W)
        t = jnp.tanh(ROOT * (acc + 0.044715 * acc * acc * acc))
        hid[part] = (0.5 * acc * (1.0 + t)).astype(BF)
        dgelu[part] = 0.5 * (1.0 + t) + 0.5 * acc * (1.0 - t * t) * (
            ROOT * (1.0 + 3 * 0.044715 * acc * acc)
        )

    def backward(part):
        slope = dot(w_out[...], gathered(1, part), 1, 0)
        d_pre[part] = (slope * dgelu[part]).astype(BF)

    rounds = []
    while 2 ** len(rounds) < M:
        rounds.append(2 ** len(rounds))

    def tell(level):
        for j in (rounds[level], N - rounds[level]):
            pl.semaphore_signal(
                reach.at[level], inc=1, device_id={"node": lax.rem(n + j, N)}, device_id_type=MESH
            )

    def hear(level):
        pl.semaphore_wait(reach.at[level], 2)

    last = len(rounds) - 1
    mix_a, mix_b = shuffle(G), shuffle(C)
    lay(0)
    lay(1)
    pl.semaphore_wait(barrier, len(peers))
    tell(0)
    y_start(0, 0)
    y_start(0, 1)
    for level in range(last):
        hear(level)
        tell(level + 1)
    y_start(1, 0)
    y_start(1, 1)
    y_to_z(0, 0)
    hear(last)
    y_to_z(0, 1)
    y_to_z(1, 0)
    y_to_z(1, 1)
    for copy in weights:
        copy.wait()
    w_out_t[...] = w_out[...].T
    bias = jnp.broadcast_to(b_in[...], (128, H)).T
    out_bias = jnp.broadcast_to(b_out[...], (128, F)).T

    unpack(0, 0)
    relay(0, 0)
    unpack(0, 1)
    relay(0, 1)
    forward(0)
    unpack(1, 0)
    sums_start(0, 0)
    forward(1)
    relay(1, 0)
    sums_middle(0, 0)
    sums_start(0, 1)
    unpack(1, 1)
    backward(0)
    sums_start(1, 0)
    relay(1, 1)
    sums_middle(0, 1)
    sums_end(0, 0)
    sums_middle(1, 0)
    backward(1)
    sums_start(1, 1)
    sums_end(0, 1)
    sums_end(1, 0)
    sums_middle(1, 1)

    ones = jnp.ones((8, 2 * W), BF)
    grad_in[...] = sum(dot(xall[0, part].reshape(D, 2 * W), d_pre[part], 1, 1) for part in range(2))
    outs = [
        pltpu.make_async_copy(grad_in, d_w_in, o_sem.at[0]),
        pltpu.make_async_copy(grad_out, d_w_out, o_sem.at[1]),
    ]
    outs[0].start()
    sums_end(1, 1)
    grad_out[...] = sum(dot(hid[part], xall[1, part].reshape(D, 2 * W), 1, 1) for part in range(2))
    outs[1].start()
    d_b_in[...] = sum(dot(ones, d_pre[part], 1, 1) for part in range(2))[0:1]
    d_b_out[...] = sum(dot(ones, xall[1, part, r], 1, 1) for part in range(2))[0:1]

    homeward(0, 0)
    homeward(0, 1)
    homeward(1, 0)
    both = landed(0)
    wide = cot[...].astype(F32)
    cut = [both[:, k * T : (k + 1) * T] for k in range(2)]
    mixed[...] = (gates[0:1, :] * cut[0] + gates[1:2, :] * cut[1]).astype(BF)
    sums = [jnp.sum(one * wide, axis=0, keepdims=True) for one in cut]
    sums = jnp.concatenate(sums + [jnp.zeros((6, T), F32)], axis=0)
    dsum[...] = sums
    shares = [
        remote(dsum, drecv.at[j - 1], p_send.at[j - 1], p_recv.at[j - 1], {"rep": lax.rem(r + j, R)})
        for j in range(1, R)
    ]
    start(shares)
    homeward(1, 1)
    arrived(shares)
    for j in range(R - 1):
        sums = sums + drecv[j]
    d_gates[...] = sums[0:2]
    d_tok[...] = landed(1).astype(BF)
    for copy in outs:
        copy.wait()
    for copy in started:
        copy.wait_send()


def hand_out(*refs):
    count = len(refs) // 3
    sources, results, held = refs[:count], refs[count : 2 * count], refs[2 * count : 3 * count]
    sem_in, sem_out = refs[3 * count :]
    parts = []
    for source, result, kept in zip(sources, results, held):
        size = source.shape[0]
        step = size // 4 if size >= 256 else size
        for i in range(0, size, step):
            span = pl.ds(i, step)
            parts.append((source.at[span], kept.at[span], result.at[span]))
    inward = [pltpu.make_async_copy(a, b, sem_in.at[i]) for i, (a, b, _) in enumerate(parts)]
    outward = [pltpu.make_async_copy(b, c, sem_out.at[i]) for i, (_, b, c) in enumerate(parts)]
    for copy in inward:
        copy.start()
    for copy, onward in zip(inward, outward):
        copy.wait()
        onward.start()
    for copy in outward:
        copy.wait()


def per_device(tokens, gates, expert_ids, w_in, b_in, w_out, b_out, cotangent):
    N, G, R = lax.axis_size("node"), lax.axis_size("grp"), lax.axis_size("rep")
    T, F = tokens.shape
    _, D, H = w_in.shape
    A, B, Q = G * CAP, G * CAP // 2, 2 * N
    W = N // 2 * B
    HF = F // 2
    dma = pltpu.SemaphoreType.DMA
    vmem = pl.BlockSpec(memory_space=pltpu.VMEM)
    any_ = pl.BlockSpec(memory_space=pl.ANY)
    shapes = (
        jax.ShapeDtypeStruct((F, T), BF),
        jax.ShapeDtypeStruct((F, T), BF),
        jax.ShapeDtypeStruct((2, T), F32),
        jax.ShapeDtypeStruct((D, H), F32),
        jax.ShapeDtypeStruct((1, H), F32),
        jax.ShapeDtypeStruct((H, D), F32),
        jax.ShapeDtypeStruct((1, F), F32),
    )
    out = pl.pallas_call(
        functools.partial(fused, N, G, R),
        out_shape=shapes,
        in_specs=[vmem, vmem, vmem, vmem, any_, vmem, any_, vmem],
        out_specs=(vmem, vmem, vmem, any_, vmem, any_, vmem),
        scratch_shapes=[
            pltpu.VMEM((N * A, 2 * T), BF),
            pltpu.VMEM((2, 2, G, Q + 16, 128), BF),
            pltpu.VMEM((2, 2, G, Q + 16, 128), BF),
            pltpu.VMEM((2, N, A + B, 128), BF),
            pltpu.VMEM((2, N, A + B, 128), BF),
            pltpu.VMEM((2, 2, R, F, 2 * W), BF),
            pltpu.VMEM((D, H), BF),
            pltpu.VMEM((H, D), BF),
            pltpu.VMEM((D, H), BF),
            pltpu.VMEM((2, H, 2 * W), F32),
            pltpu.VMEM((2, H, 2 * W), BF),
            pltpu.VMEM((2, H, 2 * W), BF),
            pltpu.VMEM((2, 2, 2, HF, 2 * W), BF),
            pltpu.VMEM((2, 2, 2, F, 2 * W), BF),
            pltpu.VMEM((2, 2, 2, HF, 2 * W), BF),
            pltpu.VMEM((2, 2, 2, F, 2 * W), BF),
            pltpu.VMEM((2, N, A + B, 128), BF),
            pltpu.VMEM((2, N, A + B, 128), BF),
            pltpu.VMEM((2, 2, G, Q + 16, 128), BF),
            pltpu.VMEM((2, 2, G, Q + 16, 128), BF),
            pltpu.VMEM((D, H), F32),
            pltpu.VMEM((H, D), F32),
            pltpu.VMEM((8, T), F32),
            pltpu.VMEM((R - 1, 8, T), F32),
            dma((2, 2, G - 1)),
            dma((2, 2, G - 1)),
            dma((2, N - 1)),
            dma((2, N - 1)),
            dma((2, 2, 3, 2)),
            dma((2, 2, 3, 2)),
            dma((2, 2, 3, 2)),
            dma((2, 2, 3, 2)),
            dma((2, N - 1)),
            dma((2, N - 1)),
            dma((2, 2, G - 1)),
            dma((2, 2, G - 1)),
            dma((R - 1,)),
            dma((R - 1,)),
            dma((4,)),
            pltpu.SemaphoreType.REGULAR((4,)),
        ],
        compiler_params=pltpu.CompilerParams(
            collective_id=0, has_side_effects=True, vmem_limit_bytes=VLIM * 2**20
        ),
    )(
        tokens.T, cotangent.T, expert_ids.T, gates.T,
        w_in[0], b_in, w_out[0], b_out,
    )
    out = pl.pallas_call(
        hand_out,
        out_shape=shapes,
        in_specs=[any_] * 7,
        out_specs=(any_,) * 7,
        scratch_shapes=[pltpu.VMEM(one.shape, one.dtype) for one in shapes] + [dma((13,)), dma((13,))],
    )(*out)
    mixed, d_tok, d_gates, d_w_in, d_b_in, d_w_out, d_b_out = out
    return (mixed.T, d_tok.T, d_gates.T, d_w_in[None], d_b_in, d_w_out[None], d_b_out)


def solution(mesh):
    both = ("node", "grp")
    return jax.shard_map(
        per_device,
        mesh=mesh,
        in_specs=(
            P(both, "rep"),
            P(both, None),
            P(both, None),
            P(both, None, "rep"),
            P(both, "rep"),
            P(both, "rep", None),
            P(both, "rep"),
            P(both, "rep"),
        ),
        out_specs=(
            P(both, "rep"),
            P(both, "rep"),
            P(both, None),
            P(both, None, "rep"),
            P(both, "rep"),
            P(both, "rep", None),
            P(both, "rep"),
        ),
        check_vma=False,
    )
```

```python
import functools
import math

import jax
import jax.numpy as jnp
from jax import lax
from jax.experimental import pallas as pl
from jax.experimental.pallas import tpu as pltpu
from jax.sharding import PartitionSpec as P

MESH = pl.DeviceIdType.MESH
CAP = 4
VLIM = 60
BF = jnp.bfloat16
F32 = jnp.float32
ROOT = math.sqrt(2.0 / math.pi)


def dot(a, b, ca, cb):
    return lax.dot_general(a, b, (((ca,), (cb,)), ((), ())), preferred_element_type=F32)


def fused(
    N, G, R,
    tok, cot, ids, gates, w_in_hbm, b_in, w_out_hbm, b_out,
    mixed, d_tok, d_gates, d_w_in, d_b_in, d_w_out, d_b_out,
    place, ysend, yrecv, zsend, zrecv, xall, w_in, w_out, w_out_t, dgelu, hid, d_pre,
    xhalf, xfull, rhalf, rfull, zback, zret, back, yret, grad_in, grad_out, dsum, drecv,
    y_send, y_recv, z_send, z_recv, x_send, x_recv, r_send, r_recv,
    s_send, s_recv, b_send, b_recv, p_send, p_recv, o_sem, reach,
):
    n, g, r = lax.axis_index("node"), lax.axis_index("grp"), lax.axis_index("rep")
    F, T = tok.shape
    D, H = w_in.shape
    A = G * CAP
    B = A // 2
    K = N // 4
    M = N // 2
    Q = 2 * N
    W = M * B
    HF, FB = F // 2, F - 128
    C = G // 2

    right_x, left_x = lax.rem(r + 1, R), lax.rem(r + R - 1, R)
    far_x = lax.rem(r + 2, R)

    barrier = pltpu.get_barrier_semaphore()
    peers = [{"node": lax.rem(n + j, N)} for j in (1, N - 1)]
    peers += [{"grp": lax.rem(g + j, G)} for j in range(1, G)]
    peers += [{"rep": lax.rem(r + j, R)} for j in range(1, R)]
    for peer in peers:
        pl.semaphore_signal(barrier, inc=1, device_id=peer, device_id_type=MESH)

    weights = [
        pltpu.make_async_copy(w_in_hbm, w_in, o_sem.at[2]),
        pltpu.make_async_copy(w_out_hbm, w_out, o_sem.at[3]),
    ]
    for copy in weights:
        copy.start()

    def remote(src, dst, send, recv, peer):
        return pltpu.make_async_remote_copy(
            src_ref=src, dst_ref=dst, send_sem=send, recv_sem=recv,
            device_id=peer, device_id_type=MESH,
        )

    started = []

    def start(copies):
        for copy in copies:
            copy.start()
        started.extend(copies)

    def arrived(copies):
        for copy in copies:
            copy.wait_recv()

    ids_i = ids[...]
    ids_f = ids_i.astype(F32)
    rows = [ids_f[k : k + 1, :] for k in range(2)]
    near_first = [0]
    for j in range(1, M):
        near_first += [j, N - j]
    near_first.append(M)
    spot = {j: i for i, j in enumerate(near_first)}
    away = lax.rem(n + 16 * N - lax.div(ids_i, G), N)
    ahead = sum(jnp.where(away == j, spot[j], 0) for j in range(1, N))
    base = (lax.rem(ids_i, G) * N + ahead) * CAP
    base = jnp.where(ids_i < N * G, base, -CAP * T).astype(F32)
    cols = [jnp.broadcast_to(row, (T, T)).T for row in rows]
    earlier = lax.broadcasted_iota(jnp.int32, (T, T), 0) < lax.broadcasted_iota(jnp.int32, (T, T), 1)
    slot = lax.broadcasted_iota(jnp.int32, (N * A, T), 0).astype(F32)
    for k in range(2):
        same = jnp.where(cols[0] == rows[k], 1.0, 0.0) + jnp.where(cols[1] == rows[k], 1.0, 0.0)
        rank = jnp.sum(jnp.where(earlier, same, 0.0), axis=0, keepdims=True)
        target = base[k : k + 1, :] + rank
        place[:, k * T : (k + 1) * T] = jnp.where(slot == target, 1.0, 0.0).astype(BF)

    @functools.cache
    def y_copies(which, part):
        return [
            remote(
                ysend.at[which, part, lax.rem(g + j, G)], yrecv.at[which, part, g],
                y_send.at[which, part, j - 1], y_recv.at[which, part, j - 1], {"grp": lax.rem(g + j, G)},
            )
            for j in sorted(range(1, G), key=lambda j: abs(j - G // 2))
        ]

    def lay(which):
        if which == 0:
            got = dot(place[:, 0:T] + place[:, T : 2 * T], tok[...], 1, 1)
        else:
            wide = cot[...].astype(F32)
            grads = [(gates[k : k + 1, :] * wide).astype(BF) for k in range(2)]
            got = dot(place[...], jnp.concatenate(grads, axis=1), 1, 1)
        got = got.reshape(G, 2, Q, F)
        for h in range(2):
            ysend[which, h, :, 0:Q] = got[:, h, :, 0:128].astype(BF)
            for w in range(K // 2):
                ysend[which, h, :, Q : Q + 16, w * FB : (w + 1) * FB] = (
                    got[:, h, w * 16 : (w + 1) * 16, 128:F].astype(BF)
                )

    def y_start(which, part):
        start(y_copies(which, part))
        yrecv[which, part, g] = ysend[which, part, g]

    def shuffle(groups):
        size = 4 * groups * CAP
        i = lax.broadcasted_iota(jnp.int32, (size, size), 0)
        j = lax.broadcasted_iota(jnp.int32, (size, size), 1)
        e, v, c = i // (4 * CAP), lax.rem(i // CAP, 4), lax.rem(i, CAP)
        return jnp.where(j == (v * groups + e) * CAP + c, 1.0, 0.0).astype(BF)

    def y_to_z(which, part):
        arrived(y_copies(which, part))
        source, target = yrecv.at[which, part], zsend.at[which]
        b = source[:, Q : Q + 16, :].reshape(4 * A, 128)
        for w in range(K // 2):
            q = part * (K // 2) + w
            a = source[:, w * 16 : w * 16 + 16, :].reshape(4 * A, 128)
            target[4 * q : 4 * q + 4, 0:A, :] = dot(mix_a, a, 0, 0).astype(BF).reshape(4, A, 128)
            for c in range(2):
                piece = dot(mix_b, b[c * 4 * B : (c + 1) * 4 * B], 0, 0)
                if c != w:
                    piece = pltpu.roll(piece, FB, 1)
                target[4 * q : 4 * q + 4, A : A + B, c * FB : (c + 1) * FB] = (
                    piece[:, c * FB : (c + 1) * FB].astype(BF).reshape(4, B, FB)
                )
        start(z_copies(which, part))
        if part == 0:
            zrecv[which, 0] = zsend[which, 0]

    def z_to_y(source, target, part):
        for w in range(K // 2):
            q = part * (K // 2) + w
            a = source[4 * q : 4 * q + 4, 0:A, :].reshape(4 * A, 128)
            target[:, w * 16 : w * 16 + 16, :] = dot(mix_a, a, 1, 0).astype(BF).reshape(G, 16, 128)
            b = dot(mix_b, source[4 * q : 4 * q + 4, A : A + B, :].reshape(4 * B, 128), 1, 0)
            turned = pltpu.roll(b, FB, 1)
            for c in range(2):
                piece = (b if c == w else turned)[:, w * FB : (w + 1) * FB]
                target[c * C : (c + 1) * C, Q : Q + 16, w * FB : (w + 1) * FB] = (
                    piece.astype(BF).reshape(C, 16, FB)
                )

    @functools.cache
    def z_copies(which, part):
        return [
            remote(
                zsend.at[which, spot[j]], zrecv.at[which, spot[j]],
                z_send.at[which, j - 1], z_recv.at[which, j - 1], {"node": lax.rem(n + N - j, N)},
            )
            for j in reversed(near_first[part * M : (part + 1) * M])
            if j
        ]

    @functools.cache
    def x_copies(which, part, stage):
        own = xall.at[which, part, r]
        top, low = own.at[pl.ds(0, HF)], own.at[pl.ds(HF, HF)]
        if stage == 0:
            pair = top, low
        elif stage == 1:
            pair = low, top
        else:
            pair = (
                xall.at[which, part, left_x, pl.ds(0, HF)],
                xall.at[which, part, right_x, pl.ds(HF, HF)],
            )
        return [
            remote(
                ref, ref, x_send.at[which, part, stage, i], x_recv.at[which, part, stage, i],
                {"rep": (right_x, left_x)[i]},
            )
            for i, ref in enumerate(pair)
        ]

    def unpack(which, part):
        arrived(z_copies(which, part))
        nodes = slice(part * M, (part + 1) * M)
        low = zrecv[which, nodes, A : A + B, :].reshape(W, 128).T
        for c in range(2):
            lanes = slice(c * W, (c + 1) * W)
            a = zrecv[which, nodes, c * B : (c + 1) * B, :].reshape(W, 128)
            xall[which, part, r, 0:128, lanes] = a.T
            xall[which, part, r, 128:F, lanes] = low[c * FB : (c + 1) * FB]
        start(x_copies(which, part, 0))
        start(x_copies(which, part, 1))

    def relay(which, part):
        for i in range(2):
            x_copies(which, part, 0)[i].wait_recv()
            start([x_copies(which, part, 2)[i]])

    def gathered(which, part):
        arrived(x_copies(which, part, 1))
        arrived(x_copies(which, part, 2))
        return xall[which, part].reshape(D, 2 * W)

    def widen(column, width):
        return jnp.concatenate([column] * (width // 128), axis=1) if width >= 128 else column[:, :width]

    @functools.cache
    def r_copies(way, part, stage):
        found = []
        for i in range(2):
            peer = {"rep": (left_x, right_x)[i]}
            if stage == 0:
                src, dst = xhalf.at[way, part, i], rhalf.at[way, part, i]
            else:
                span = pl.ds(HF if (i == 0) == (stage == 1) else 0, HF)
                src, dst = xfull.at[way, part, i, span], rfull.at[way, part, i, span]
            found.append(
                remote(src, dst, r_send.at[way, part, stage, i], r_recv.at[way, part, stage, i], peer)
            )
        return found

    def partial(way, part, target):
        span = pl.ds(pl.multiple_of(target * F, F), F)
        if way == 0:
            return dot(w_out_t[span, :], hid[part], 1, 0)
        return dot(w_in[span, :], d_pre[part], 1, 0)

    def sums_start(way, part):
        far = partial(way, part, far_x).astype(BF)
        xhalf[way, part, 0] = far[0:HF]
        xhalf[way, part, 1] = far[HF:F]
        start(r_copies(way, part, 0))
        for i, target in ((0, left_x), (1, right_x)):
            xfull[way, part, i] = partial(way, part, target).astype(BF)
            start([r_copies(way, part, 1)[i]])

    def sums_middle(way, part):
        for i in range(2):
            r_copies(way, part, 0)[i].wait_recv()
            span = slice(0, HF) if i == 0 else slice(HF, F)
            total = xfull[way, part, i, span].astype(F32) + rhalf[way, part, i].astype(F32)
            xfull[way, part, i, span] = total.astype(BF)
            start([r_copies(way, part, 2)[i]])

    @functools.cache
    def s_copies(way, part):
        return [
            remote(
                zback.at[way, spot[j]], zret.at[way, spot[j]],
                s_send.at[way, j - 1], s_recv.at[way, j - 1], {"node": lax.rem(n + j, N)},
            )
            for j in reversed(near_first[part * M : (part + 1) * M])
            if j
        ]

    def sums_end(way, part):
        total = partial(way, part, r)
        if way == 0:
            total = total + widen(out_bias, 2 * W)
        for i in range(2):
            r_copies(way, part, 1)[i].wait_recv()
            r_copies(way, part, 2)[i].wait_recv()
            total = total + rfull[way, part, i].astype(F32)
        value = total.astype(BF)
        nodes = slice(part * M, (part + 1) * M)
        low = jnp.concatenate([value[128:F, 0:W], value[128:F, W : 2 * W]], axis=0)
        zback[way, nodes, A : A + B, :] = low.T.reshape(M, B, 128)
        for c in range(2):
            zback[way, nodes, c * B : (c + 1) * B, :] = (
                value[0:128, c * W : (c + 1) * W].T.reshape(M, B, 128)
            )
        start(s_copies(way, part))
        if part == 0:
            zret[way, 0] = zback[way, 0]

    @functools.cache
    def b_copies(way, part):
        return [
            remote(
                back.at[way, part, lax.rem(g + j, G)], yret.at[way, part, g],
                b_send.at[way, part, j - 1], b_recv.at[way, part, j - 1], {"grp": lax.rem(g + j, G)},
            )
            for j in sorted(range(1, G), key=lambda j: abs(j - G // 2))
        ]

    def homeward(way, part):
        arrived(s_copies(way, part))
        z_to_y(zret.at[way], back.at[way, part], part)
        start(b_copies(way, part))
        yret[way, part, g] = back[way, part, g]

    def landed(way):
        hot = place[...] if way == 0 else place[:, 0:T] + place[:, T : 2 * T]
        width = hot.shape[1]
        hot = hot.reshape(G, 2, Q, width)
        top, rest = 0.0, 0.0
        for h in (0, 1):
            arrived(b_copies(way, h))
            top += dot(yret[way, h, :, 0:Q].reshape(G * Q, 128), hot[:, h].reshape(G * Q, width), 0, 0)
            low = yret[way, h, :, Q : Q + 16].reshape(G * 16, 128)
            for w in range(K // 2):
                one = hot[:, h, w * 16 : (w + 1) * 16].reshape(G * 16, width)
                rest += dot(low, one, 0, 0)[w * FB : (w + 1) * FB]
        return jnp.concatenate([top, rest], axis=0)

    def forward(part):
        x = gathered(0, part)
        acc = dot(w_in[...], x, 0, 0) + widen(bias, 2 * W)
        t = jnp.tanh(ROOT * (acc + 0.044715 * acc * acc * acc))
        hid[part] = (0.5 * acc * (1.0 + t)).astype(BF)
        dgelu[part] = 0.5 * (1.0 + t) + 0.5 * acc * (1.0 - t * t) * (
            ROOT * (1.0 + 3 * 0.044715 * acc * acc)
        )

    def backward(part):
        slope = dot(w_out[...], gathered(1, part), 1, 0)
        d_pre[part] = (slope * dgelu[part]).astype(BF)

    rounds = []
    while 2 ** len(rounds) < M:
        rounds.append(2 ** len(rounds))

    def tell(level):
        for j in (rounds[level], N - rounds[level]):
            pl.semaphore_signal(
                reach.at[level], inc=1, device_id={"node": lax.rem(n + j, N)}, device_id_type=MESH
            )

    def hear(level):
        pl.semaphore_wait(reach.at[level], 2)

    last = len(rounds) - 1
    mix_a, mix_b = shuffle(G), shuffle(C)
    lay(0)
    lay(1)
    pl.semaphore_wait(barrier, len(peers))
    tell(0)
    y_start(0, 0)
    y_start(0, 1)
    for level in range(last):
        hear(level)
        tell(level + 1)
    y_start(1, 0)
    y_start(1, 1)
    y_to_z(0, 0)
    hear(last)
    y_to_z(0, 1)
    y_to_z(1, 0)
    y_to_z(1, 1)
    for copy in weights:
        copy.wait()
    w_out_t[...] = w_out[...].T
    bias = jnp.broadcast_to(b_in[...], (128, H)).T
    out_bias = jnp.broadcast_to(b_out[...], (128, F)).T

    unpack(0, 0)
    relay(0, 0)
    unpack(0, 1)
    relay(0, 1)
    forward(0)
    unpack(1, 0)
    sums_start(0, 0)
    forward(1)
    relay(1, 0)
    sums_middle(0, 0)
    sums_start(0, 1)
    unpack(1, 1)
    backward(0)
    sums_start(1, 0)
    relay(1, 1)
    sums_middle(0, 1)
    sums_end(0, 0)
    sums_middle(1, 0)
    backward(1)
    sums_start(1, 1)
    sums_end(0, 1)
    sums_end(1, 0)
    sums_middle(1, 1)

    ones = jnp.ones((8, 2 * W), BF)
    grad_in[...] = sum(dot(xall[0, part].reshape(D, 2 * W), d_pre[part], 1, 1) for part in range(2))
    outs = [
        pltpu.make_async_copy(grad_in, d_w_in, o_sem.at[0]),
        pltpu.make_async_copy(grad_out, d_w_out, o_sem.at[1]),
    ]
    outs[0].start()
    sums_end(1, 1)
    grad_out[...] = sum(dot(hid[part], xall[1, part].reshape(D, 2 * W), 1, 1) for part in range(2))
    outs[1].start()
    d_b_in[...] = sum(dot(ones, d_pre[part], 1, 1) for part in range(2))[0:1]
    d_b_out[...] = sum(dot(ones, xall[1, part, r], 1, 1) for part in range(2))[0:1]

    homeward(0, 0)
    homeward(0, 1)
    homeward(1, 0)
    both = landed(0)
    wide = cot[...].astype(F32)
    cut = [both[:, k * T : (k + 1) * T] for k in range(2)]
    mixed[...] = (gates[0:1, :] * cut[0] + gates[1:2, :] * cut[1]).astype(BF)
    sums = [jnp.sum(one * wide, axis=0, keepdims=True) for one in cut]
    sums = jnp.concatenate(sums + [jnp.zeros((6, T), F32)], axis=0)
    dsum[...] = sums
    shares = [
        remote(dsum, drecv.at[j - 1], p_send.at[j - 1], p_recv.at[j - 1], {"rep": lax.rem(r + j, R)})
        for j in range(1, R)
    ]
    start(shares)
    homeward(1, 1)
    arrived(shares)
    for j in range(R - 1):
        sums = sums + drecv[j]
    d_gates[...] = sums[0:2]
    d_tok[...] = landed(1).astype(BF)
    for copy in outs:
        copy.wait()
    for copy in started:
        copy.wait_send()


def hand_out(*refs):
    count = len(refs) // 3
    sources, results, held = refs[:count], refs[count : 2 * count], refs[2 * count : 3 * count]
    sem_in, sem_out = refs[3 * count :]
    parts = []
    for source, result, kept in zip(sources, results, held):
        size = source.shape[0]
        step = size // 4 if size >= 256 else size
        for i in range(0, size, step):
            span = pl.ds(i, step)
            parts.append((source.at[span], kept.at[span], result.at[span]))
    inward = [pltpu.make_async_copy(a, b, sem_in.at[i]) for i, (a, b, _) in enumerate(parts)]
    outward = [pltpu.make_async_copy(b, c, sem_out.at[i]) for i, (_, b, c) in enumerate(parts)]
    for copy in inward:
        copy.start()
    for copy, onward in zip(inward, outward):
        copy.wait()
        onward.start()
    for copy in outward:
        copy.wait()


def per_device(tokens, gates, expert_ids, w_in, b_in, w_out, b_out, cotangent):
    N, G, R = lax.axis_size("node"), lax.axis_size("grp"), lax.axis_size("rep")
    T, F = tokens.shape
    _, D, H = w_in.shape
    A, B, Q = G * CAP, G * CAP // 2, 2 * N
    W = N // 2 * B
    HF = F // 2
    dma = pltpu.SemaphoreType.DMA
    vmem = pl.BlockSpec(memory_space=pltpu.VMEM)
    any_ = pl.BlockSpec(memory_space=pl.ANY)
    shapes = (
        jax.ShapeDtypeStruct((F, T), BF),
        jax.ShapeDtypeStruct((F, T), BF),
        jax.ShapeDtypeStruct((2, T), F32),
        jax.ShapeDtypeStruct((D, H), F32),
        jax.ShapeDtypeStruct((1, H), F32),
        jax.ShapeDtypeStruct((H, D), F32),
        jax.ShapeDtypeStruct((1, F), F32),
    )
    out = pl.pallas_call(
        functools.partial(fused, N, G, R),
        out_shape=shapes,
        in_specs=[vmem, vmem, vmem, vmem, any_, vmem, any_, vmem],
        out_specs=(vmem, vmem, vmem, any_, vmem, any_, vmem),
        scratch_shapes=[
            pltpu.VMEM((N * A, 2 * T), BF),
            pltpu.VMEM((2, 2, G, Q + 16, 128), BF),
            pltpu.VMEM((2, 2, G, Q + 16, 128), BF),
            pltpu.VMEM((2, N, A + B, 128), BF),
            pltpu.VMEM((2, N, A + B, 128), BF),
            pltpu.VMEM((2, 2, R, F, 2 * W), BF),
            pltpu.VMEM((D, H), BF),
            pltpu.VMEM((H, D), BF),
            pltpu.VMEM((D, H), BF),
            pltpu.VMEM((2, H, 2 * W), F32),
            pltpu.VMEM((2, H, 2 * W), BF),
            pltpu.VMEM((2, H, 2 * W), BF),
            pltpu.VMEM((2, 2, 2, HF, 2 * W), BF),
            pltpu.VMEM((2, 2, 2, F, 2 * W), BF),
            pltpu.VMEM((2, 2, 2, HF, 2 * W), BF),
            pltpu.VMEM((2, 2, 2, F, 2 * W), BF),
            pltpu.VMEM((2, N, A + B, 128), BF),
            pltpu.VMEM((2, N, A + B, 128), BF),
            pltpu.VMEM((2, 2, G, Q + 16, 128), BF),
            pltpu.VMEM((2, 2, G, Q + 16, 128), BF),
            pltpu.VMEM((D, H), F32),
            pltpu.VMEM((H, D), F32),
            pltpu.VMEM((8, T), F32),
            pltpu.VMEM((R - 1, 8, T), F32),
            dma((2, 2, G - 1)),
            dma((2, 2, G - 1)),
            dma((2, N - 1)),
            dma((2, N - 1)),
            dma((2, 2, 3, 2)),
            dma((2, 2, 3, 2)),
            dma((2, 2, 3, 2)),
            dma((2, 2, 3, 2)),
            dma((2, N - 1)),
            dma((2, N - 1)),
            dma((2, 2, G - 1)),
            dma((2, 2, G - 1)),
            dma((R - 1,)),
            dma((R - 1,)),
            dma((4,)),
            pltpu.SemaphoreType.REGULAR((4,)),
        ],
        compiler_params=pltpu.CompilerParams(
            collective_id=0, has_side_effects=True, vmem_limit_bytes=VLIM * 2**20
        ),
    )(
        tokens.T, cotangent.T, expert_ids.T, gates.T,
        w_in[0], b_in, w_out[0], b_out,
    )
    out = pl.pallas_call(
        hand_out,
        out_shape=shapes,
        in_specs=[any_] * 7,
        out_specs=(any_,) * 7,
        scratch_shapes=[pltpu.VMEM(one.shape, one.dtype) for one in shapes] + [dma((13,)), dma((13,))],
    )(*out)
    mixed, d_tok, d_gates, d_w_in, d_b_in, d_w_out, d_b_out = out
    return (mixed.T, d_tok.T, d_gates.T, d_w_in[None], d_b_in, d_w_out[None], d_b_out)


def solution(mesh):
    both = ("node", "grp")
    return jax.shard_map(
        per_device,
        mesh=mesh,
        in_specs=(
            P(both, "rep"),
            P(both, None),
            P(both, None),
            P(both, None, "rep"),
            P(both, "rep"),
            P(both, "rep", None),
            P(both, "rep"),
            P(both, "rep"),
        ),
        out_specs=(
            P(both, "rep"),
            P(both, "rep"),
            P(both, None),
            P(both, None, "rep"),
            P(both, "rep"),
            P(both, "rep", None),
            P(both, "rep"),
        ),
        check_vma=False,
    )
```
